256 devices in a mesh: row: 8 (over z), col: 32 (over x, y, core).
Axes of the slice: x: 4, y: 4, z: 8, core: 2. Of those that a mesh axis runs over, the one named last changes fastest.
Arguments:
- forcing: float32 [3, 4096, 128], P(None, ('row', 'col')), may hold values from -27 to 27
- stiffness: float32 [4096], P(('row', 'col')), may hold values from 0.02 to 0.3
- positions: float32 [3, 4096], P(None, ('row', 'col')), may hold values from 0 to 1
- far_weights: float32 [128], replicated, may hold values from 0 to 0.015625
- far_profile: float32 [128], replicated, may hold values from 0.5 to 1.5
- near_blocks: bfloat16 [8192, 384, 384], P(('row', 'col')), may hold values from -0.125 to 0.125
- near_dest: int32 [8192, 1], P(('row', 'col')), may hold values from 0 to 31; in each aligned block of 32 rows (0 to 31, 32 to 63, ...) at most 2 rows name the same one
- near_cilia: int32 [8192, 2], P(('row', 'col')), may hold values from 0 to 15
- near_count: int32 [256], P(('row', 'col')), may hold values from 16 to 32, as said below
Outputs:
- solution: float32 [3, 4096, 128], P(None, ('row', 'col'))
- residual: float32 [3, 4096, 128], P(None, ('row', 'col'))
The draws below stay inside these ranges and needn't reach their ends.
Inputs may be any that keep to these rules, and one draw needn't show every extreme that they name: `near_dest`: among the 32 slots of one device no index of col is named more than 2 times, and in every draw some device names one exactly 2 times. `near_cilia`: column 0 is the source cilium's place among its device's 16 cilia, column 1 the target cilium's place on its device. `near_count`: some device has all 32 slots live.
All inputs are finite; a program needn't handle non-finite values.
Results may differ from the reference program's by a relative error of at most 0.01.
Values may be sent and summed in bfloat16 or wider, within the bound.
No kernel may reach another device: no remote copies, remote signals or barrier semaphores. Data moves between devices by JAX's collectives and lax.ppermute only.
A program may use at most 192 MiB of HBM per device.

```python
import math
import jax
import jax.numpy as jnp
import numpy as np
from jax import lax

Q = 128
CIL = 16
CAPD = 2
ITERS = 4
NB = 32
CILIA = 4096
N_ROW = 8
N_COL = 32


def draw_forcing(key, part):
    first_key, second_key = jax.random.split(key)
    rising = jnp.exp(jnp.log(3.0) * jnp.arange(CILIA, dtype=jnp.float32) / CILIA)
    roughness = jax.random.uniform(second_key, (CILIA,), jnp.float32, 0.5, 1.5)
    values = jnp.clip(jax.random.normal(first_key, (3, CILIA, Q), jnp.float32), -4.0, 4.0)
    scales = rising * roughness
    return values * scales[None, :, None]


def draw_near_count(key, part):
    first_key, second_key = jax.random.split(key)
    device_total = CILIA // CIL
    counts = jax.random.randint(first_key, (device_total,), NB // 2, NB + 1)
    chosen = jax.random.randint(second_key, (), 0, device_total)
    return jnp.where(jnp.arange(device_total) == chosen, NB, counts).astype(jnp.int32)


def place_ends(result, stream_key, smallest, top_value):
    extent = result.shape
    index_at = [jax.random.randint(jax.random.fold_in(stream_key, axis), (), 0, extent[axis]) for axis in range(len(extent))]
    result = result.at[tuple(index_at)].set(smallest)
    longest = extent.index(max(extent))
    index_at[longest] = (index_at[longest] + 1) % extent[longest]
    return result.at[tuple(index_at)].set(top_value)


def block_scale(own_key, dims, cuts, smallest, largest):
    def one(dim, parts):
        steps = jax.random.uniform(jax.random.fold_in(jax.random.fold_in(own_key, 6), dim), (parts,), jnp.float32, smallest / len(cuts), largest / len(cuts))
        return jnp.repeat(jnp.exp(steps), dims[dim] // parts).reshape((-1,) + (1,) * (len(dims) - dim - 1))

    level = one(*cuts[0])
    for cut in cuts[1:]:
        level = level * one(*cut)
    return level


def shared_out(key, own, number, rows, count, top, bound, skew):
    ranking = jax.random.permutation(key, count)
    packed, common = shares(count, rows * top, bound, skew, True), shares(count, rows * top, bound, skew, False)
    places = jnp.arange(count)

    def named(sizes, rotation):
        used = int((sizes > 0).sum())
        fixed = max(1, used // 4)
        passed = fixed + (places - fixed + rotation * (used - fixed)) % max(1, count - fixed)
        return jnp.zeros((count,), jnp.int32).at[ranking[jnp.where(places < fixed, places, passed)]].set(jnp.asarray(sizes, jnp.int32))

    sizes = jnp.where(number % 4 == 0, named(packed, number // 4), named(common, number - number // 4 - 1))
    mixed = jax.random.permutation(jax.random.fold_in(own, 3), count)
    donor, sink = mixed[0:count // 2 * 2:2], mixed[1:count // 2 * 2:2]
    room = jnp.minimum(sizes[donor] - 1, bound - sizes[sink]) // 2
    room = jnp.where((donor == ranking[0]) | (sink == ranking[0]) | (sizes[sink] == 0), 0, jnp.maximum(room, 0))
    passed = jax.random.randint(jax.random.fold_in(own, 4), (count // 2,), 0, 1 << 20) % (room + 1)
    sizes = sizes.at[donor].add(-passed).at[sink].add(passed)
    labels = jnp.searchsorted(jnp.cumsum(sizes), jnp.arange(rows * top), side="right").astype(jnp.int32)
    table = labels.reshape(top, rows).T
    table = table[jax.random.permutation(jax.random.fold_in(own, 1), rows)]
    rotation = jax.random.randint(jax.random.fold_in(own, 2), (rows, 1), 0, top)
    return jnp.take_along_axis(table, (jnp.arange(top)[None, :] + rotation) % top, axis=1)


def shares(count, total, most, lean, full):
    loads = [(1 << 20) // math.isqrt(standing ** lean) + 1 for standing in range(1, count + 1)]
    largest = most if full else min(most, max(-(-total // count), total * loads[0] // sum(loads)))
    least = 1 if total - largest >= count - 1 else 0
    given, spare = [largest] + [least] * (count - 1), total - largest - least * (count - 1)
    while spare > 0:
        movable = [i for i in range(1, count) if given[i] < largest] or [i for i in range(1, count) if given[i] < most]
        whole, left = sum([loads[i] for i in movable]), spare
        for i in movable:
            addition = min(most - given[i], max(1, left * loads[i] // whole), spare)
            given[i] = given[i] + addition
            spare = spare - addition
    return np.array(given)


def normal_values(own_key, dims, spread, limit, pieces=(), held_as=jnp.bfloat16):
    values = jax.random.normal(own_key, dims, jnp.float32) * spread
    if len(pieces) > 0:
        values = block_scale(own_key, dims, pieces, -0.22, 0.18) * values
    return jnp.clip(values, min=-limit, max=limit).astype(held_as)


def setup_inputs(seed: int = 0) -> dict:
    key_list = jax.random.split(jax.random.key(seed), 10)
    forcing = draw_forcing(jax.random.fold_in(key_list[9], 71), 0)
    stiffness = jnp.clip(jnp.exp(math.log(0.3) - 2.7080503 * jax.random.uniform(key_list[1], (CILIA,), jnp.float32) ** block_scale(key_list[1], (CILIA,), ((0, 256),), -0.2, 0.2)), 0.02, 0.3)
    positions = jnp.clip(1.0 * jax.random.uniform(key_list[2], (3, CILIA), jnp.float32) ** block_scale(key_list[2], (3, CILIA), ((1, 256),), -0.2, 0.2), 0.0, 1.0)
    far_weights = jnp.clip(jax.random.uniform(key_list[3], (Q,), jnp.float32, 0.0, 0.015625), 0.0, 0.015625)
    far_profile = jnp.clip(jax.random.uniform(key_list[4], (Q,), jnp.float32, 0.5, 1.5), 0.5, 1.5)
    near_blocks = normal_values(key_list[5], (N_ROW * N_COL * NB, 3 * Q, 3 * Q), (18.75 * Q) ** -0.5, 0.125, ((0, 256),))
    near_dest_keys = jax.random.split(jax.random.fold_in(key_list[6], 1), (N_ROW * N_COL * NB) // NB)
    near_dest_turns = jax.random.permutation(jax.random.fold_in(key_list[6], 3), (N_ROW * N_COL * NB) // NB)
    near_dest = jax.vmap(lambda own, number: shared_out(jax.random.fold_in(key_list[6], 2), own, number, NB, N_COL, 1, CAPD, 2))(near_dest_keys, near_dest_turns).reshape((N_ROW * N_COL * NB, 1))
    near_cilia = place_ends(jax.random.randint(key_list[7], (N_ROW * N_COL * NB, 2), 0, CIL), jax.random.fold_in(key_list[7], 1), 0, CIL - 1).astype(jnp.int32)
    near_count = draw_near_count(jax.random.fold_in(key_list[9], 71), 0)
    return dict(forcing=forcing, stiffness=stiffness, positions=positions, far_weights=far_weights, far_profile=far_profile, near_blocks=near_blocks, near_dest=near_dest, near_cilia=near_cilia, near_count=near_count)


EPSILON = 1e-06

def bending(vector, stiffness):
    padded = jnp.pad(vector, ((0, 0), (0, 0), (2, 2)))
    fourth = padded[:, :, :-4] - 4.0 * padded[:, :, 1:-3] + 6.0 * vector - 4.0 * padded[:, :, 3:-1] + padded[:, :, 4:]
    return vector + stiffness[None, :, None] * fourth

def far_block(target_pos, source_pos, strengths, eps_two, eps_three):
    displacement = target_pos[:, :, None] - source_pos[:, None, :]
    inverse = 1.0 / (lax.optimization_barrier(jnp.sum(displacement * displacement, axis=0)) + eps_two)
    amplitude = eps_three * inverse * jnp.sqrt(inverse)
    projected = lax.optimization_barrier(jnp.sum(displacement * strengths[:, None, :], axis=0)) * inverse
    return lax.optimization_barrier(jnp.sum(amplitude[None] * (strengths[:, None, :] + displacement * projected[None]), axis=2))

def far_field(vector, positions, far_weights, far_profile):
    strengths = lax.optimization_barrier(jnp.sum(vector * far_weights[None, None, :], axis=2))
    eps_three = 4.0 / CILIA
    eps_two = eps_three ** (2.0 / 3.0)
    block_size = min(CILIA, 256)
    target_tiles = positions.reshape(3, CILIA // block_size, block_size).transpose(1, 0, 2)

    def one_tile(target_pos):
        return far_block(target_pos, positions, strengths, eps_two, eps_three)
    speeds = lax.map(one_tile, target_tiles)
    speeds = speeds.transpose(1, 0, 2).reshape(3, CILIA)
    return speeds[:, :, None] * far_profile[None, None, :]

def near_field(vector, near_blocks, near_dest, near_cilia, near_count):
    device_total = CILIA // CIL
    row_table = vector.transpose(1, 0, 2).reshape(CILIA, 3 * Q)
    slot_ids = jnp.arange(device_total * NB, dtype=jnp.int32)
    owner = slot_ids // NB
    active = slot_ids % NB < near_count[owner]
    source_ids = owner * CIL + near_cilia[:, 0]
    target_ids = (owner // N_COL * N_COL + near_dest[:, 0]) * CIL + near_cilia[:, 1]
    picked = row_table[source_ids].astype(jnp.bfloat16).reshape(device_total, NB, 3 * Q)

    def one_device(pair):
        blocks, inputs = pair
        return jnp.einsum('kij,kj->ki', blocks.astype(jnp.float32), inputs.astype(jnp.float32))
    speeds = lax.map(one_device, (near_blocks.reshape(device_total, NB, 3 * Q, 3 * Q), picked))
    speeds = speeds.reshape(device_total * NB, 3 * Q)
    speeds = jnp.where(active[:, None], speeds, 0.0)
    summed = jnp.zeros((CILIA, 3 * Q), jnp.float32).at[target_ids].add(speeds)
    return summed.reshape(CILIA, 3, Q).transpose(1, 0, 2)

def back_substitute(triangle, target):
    answers = [None] * ITERS
    for index in reversed(range(ITERS)):
        running = target[index]
        for later in range(index + 1, ITERS):
            running = running - triangle[index, later] * answers[later]
        answers[index] = running / triangle[index, index]
    return jnp.stack(answers)

def least_squares(hessenberg, initial_norm):
    unit_columns = []
    triangle = jnp.zeros((ITERS, ITERS), jnp.float32)
    for column in range(ITERS):
        vector = hessenberg[:, column]
        for earlier in range(column):
            weight = jnp.sum(unit_columns[earlier] * vector)
            triangle = triangle.at[earlier, column].set(weight)
            vector = vector - weight * unit_columns[earlier]
        length = jnp.sqrt(jnp.sum(vector * vector))
        triangle = triangle.at[column, column].set(length)
        unit_columns.append(vector / length)
    target = initial_norm * jnp.stack([unit[0] for unit in unit_columns])
    return back_substitute(triangle, target)

def reference(forcing, stiffness, positions, far_weights, far_profile, near_blocks, near_dest, near_cilia, near_count):

    def operator(vector):
        return bending(vector, stiffness) + near_field(vector, near_blocks, near_dest, near_cilia, near_count) + far_field(vector, positions, far_weights, far_profile)
    initial_norm = jnp.sqrt(jnp.sum(forcing * forcing) + EPSILON)
    basis = [forcing / initial_norm]
    hessenberg = jnp.zeros((ITERS + 1, ITERS), jnp.float32)
    for column in range(ITERS):
        image = operator(basis[column])
        heights = [jnp.sum(basis[earlier] * image) for earlier in range(column + 1)]
        for earlier in range(column + 1):
            image = image - heights[earlier] * basis[earlier]
            hessenberg = hessenberg.at[earlier, column].set(heights[earlier])
        length = jnp.sqrt(jnp.sum(image * image) + EPSILON)
        hessenberg = hessenberg.at[column + 1, column].set(length)
        basis.append(image / length)
    coefficients = least_squares(hessenberg, initial_norm)
    solution = coefficients[0] * basis[0]
    for column in range(1, ITERS):
        solution = solution + coefficients[column] * basis[column]
    residual = forcing - operator(solution)
    return (solution, residual)
```

```python
import functools
import jax
import jax.numpy as jnp
from jax import lax
from jax.experimental import pallas as pl
from jax.experimental.pallas import tpu as pltpu
from jax.sharding import PartitionSpec as P

CAPD = 2
ITERS = 4
EPSILON = 1e-06
F32 = jnp.float32
BF16 = jnp.bfloat16
HIGHEST = lax.Precision.HIGHEST
LANES = 128
GRAM = {(j, l): l * (l + 1) // 2 + j for l in range(ITERS) for j in range(l + 1)}
HESS = {(j, k): 16 + 8 * k + j for k in range(ITERS) for j in range(k + 2)}
BETA = 63
SHIFT = 2.0


def lane_iota(shape):
    return lax.broadcasted_iota(jnp.int32, shape, len(shape) - 1)


def column(row, size):
    eye = lax.broadcasted_iota(jnp.int32, (size, size), 0) == lane_iota((size, size))
    return jnp.sum(jnp.where(eye, row, 0.0), axis=1, keepdims=True)


def tall(col, comps):
    return jnp.concatenate([col] * comps, axis=0)


def bend(x, stiff):
    points = x.shape[1]
    lane = lane_iota(x.shape)

    def shifted(by):
        moved = pltpu.roll(x, by % points, 1)
        keep = lane >= by if by > 0 else lane < points + by
        return jnp.where(keep, moved, 0.0)

    fourth = shifted(2) - 4.0 * shifted(1) + 6.0 * x - 4.0 * shifted(-1) + shifted(-2)
    return x + stiff * fourth


def placed(x, weights, place, comps, cil):
    sums = jnp.sum(x * weights, axis=1, keepdims=True)
    return [
        jnp.sum(sums[i * cil:(i + 1) * cil] * place, axis=0, keepdims=True) for i in range(comps)
    ]


def place_of(cil):
    shape = (cil, LANES)
    own = lax.axis_index("row") * cil + lax.broadcasted_iota(jnp.int32, shape, 0)
    return jnp.where(lane_iota(shape) == own, 1.0, 0.0)


def to_every(send_ref, parts):
    rows = list(parts)
    rows += [jnp.zeros((1, LANES), F32)] * (send_ref.shape[1] - len(rows))
    tile = jnp.concatenate(rows, axis=0)
    send_ref[...] = jnp.broadcast_to(tile[None], send_ref.shape)


def dot_row(pairs):
    rows = [jnp.sum(a * b, axis=0, keepdims=True) for a, b in pairs]
    while len(rows) % 8:
        rows.append(jnp.zeros_like(rows[0]))
    sums = jnp.sum(jnp.concatenate(rows, axis=0), axis=1, keepdims=True)
    shape = (len(rows), LANES)
    eye = lax.broadcasted_iota(jnp.int32, shape, 0) == lane_iota(shape)
    return jnp.sum(jnp.where(eye, sums, 0.0), axis=0, keepdims=True)


def pick(row, lane):
    return row[:, lane:lane + 1]


def pack(entries):
    lane = lane_iota((1, LANES))
    row = jnp.zeros((1, LANES), F32)
    for where, value in entries.items():
        row = jnp.where(lane == where, value, row)
    return row


def first_kernel(comps, cil, f_ref, pos_ref, w_ref, send_ref):
    f = f_ref[...]
    place = place_of(cil)
    parts = placed(f, w_ref[...], place, comps, cil)
    parts.append(dot_row([(f, f)]))
    for i in range(comps):
        col = column(pos_ref[i:i + 1, :], cil)
        parts.append(jnp.sum(col * place, axis=0, keepdims=True))
    to_every(send_ref, parts)


TILE = 8
META = 6
DOTS = 14
PITCH = {True: 24, False: 16}


def near_kernel(comps, cil, chunk, first, cilia_ref, dest_ref, count_ref, x_ref, b_ref, out_ref,
                lhs, result, used, held, sems):
    points = x_ref.shape[1]
    slots = b_ref.shape[0]

    def fetch(at):
        part = pl.ds(at * chunk, chunk)
        return pltpu.make_async_copy(b_ref.at[part], held.at[part], sems.at[at])

    for at in range(slots // chunk):
        fetch(at).start()
    result[...] = jnp.zeros_like(result)

    def clear(i, carry):
        used[i] = 0
        return carry

    lax.fori_loop(0, used.shape[0], clear, 0)
    x = x_ref[...]
    high = x.astype(BF16).astype(F32)
    low = x - high
    row = lax.broadcasted_iota(jnp.int32, (TILE, points), 0)
    for g in range(cil):
        for i in range(comps):
            at = i * cil + g
            value = jnp.where(row == 0, high[at:at + 1], jnp.where(row == 1, low[at:at + 1], 0.0))
            lhs[g, :, i * points:(i + 1) * points] = value.astype(BF16)
    lane = lane_iota((1, points))
    for at in range(slots // chunk):
        fetch(at).wait()
        speeds = [
            lax.dot_general(
                lhs[cilia_ref[0, slot]], held[slot], (((1,), (1,)), ((), ())),
                preferred_element_type=F32,
            )
            for slot in range(at * chunk, (at + 1) * chunk)
        ]
        for s in range(chunk):
            slot = at * chunk + s
            dest = dest_ref[slot]
            rank = used[dest]
            used[dest] = rank + 1
            live = slot < count_ref[0]
            speed = jnp.where(live, speeds[s][0:1] + speeds[s][1:2], 0.0)
            for i in range(comps):
                result[dest, pl.ds(rank * comps + i, 1), :] = speed[:, i * points:(i + 1) * points]
            if first:
                target = cilia_ref[1, slot].astype(F32)
                before = result[dest, META:META + 1, :]
                result[dest, META:META + 1, :] = jnp.where(lane == rank, target, before)
    out_ref[...] = result[...].astype(BF16)


def join_kernel(comps, first, rows_ref, near_ref, send_ref):
    total = jnp.sum(rows_ref[...], axis=0)
    high = total.astype(BF16).astype(F32)
    rest = total - high
    middle = rest.astype(BF16).astype(F32)
    low = rest - middle
    at = comps
    shared = jnp.concatenate(
        [
            high[:at], rest[:at], high[at:at + 1],
            middle[at:at + 1] + pltpu.roll(low[at:at + 1], LANES // 2, 1),
        ],
        axis=0,
    )
    send_ref[:, :TILE, :] = near_ref[...]
    send_ref[:, TILE:2 * TILE, :] = jnp.broadcast_to(
        shared.astype(BF16)[None], (send_ref.shape[0],) + shared.shape
    )
    if first:
        at = comps + 1
        places = jnp.concatenate(
            [high[at:at + comps], rest[at:at + comps], jnp.zeros((TILE - 2 * comps, LANES), F32)], axis=0
        )
        send_ref[:, 2 * TILE:3 * TILE, :] = jnp.broadcast_to(
            places.astype(BF16)[None], (send_ref.shape[0],) + places.shape
        )


def sorting(comps, cil, sources, pitch, targets):
    def parts(rows):
        shape = (rows, sources * pitch)
        row = lax.broadcasted_iota(jnp.int32, shape, 0)
        lane = lane_iota(shape)
        return row, lax.div(lane, pitch), lax.rem(lane, pitch)

    row, _, place = parts(comps * cil)
    comp, cilium = lax.div(row, cil), lax.rem(row, cil).astype(F32)
    found = jnp.zeros(row.shape, jnp.bool_)
    for rank in range(CAPD):
        found |= (place == rank * comps + comp) & (cilium == targets[rank])
    pieces = [found]

    def gathered(start):
        row, source, place = parts(comps * sources)
        comp, wanted = lax.div(row, sources), lax.rem(row, sources)
        here = (place == start + comp) | (place == start + comps + comp)
        return here & (source == wanted)

    pieces.append(gathered(TILE))
    row, _, place = parts(TILE)
    pieces.append((row == 0) & ((place == DOTS) | (place == DOTS + 1)))
    if pitch > 2 * TILE:
        pieces.append(gathered(2 * TILE))
    return jnp.concatenate([jnp.where(p, 1.0, 0.0) for p in pieces], axis=0).astype(BF16)


def applied(x, stiff, rows, pairs, profile, comps, cil, sources):
    flat = comps * cil
    image = bend(x, stiff) + rows[:flat]
    totals = [jnp.zeros((cil, LANES), F32) for _ in range(comps)]
    for s in range(sources):
        strength = [rows[flat + j * sources + s:flat + j * sources + s + 1] for j in range(comps)]
        for (i, j), at in PAIRS.items():
            block = pairs(at, s)
            totals[i] = totals[i] + block * strength[j]
            if i != j:
                totals[j] = totals[j] + block * strength[i]
    far = jnp.concatenate([jnp.sum(t, axis=1, keepdims=True) for t in totals], axis=0)
    dots = rows[flat + comps * sources:flat + comps * sources + 1]
    dots = dots + pltpu.roll(dots, LANES // 2, 1)
    return image + far * profile, dots


PAIRS = {(0, 0): 0, (0, 1): 1, (0, 2): 2, (1, 1): 3, (1, 2): 4, (2, 2): 5}


def krylov_kernel(comps, cil, sources, total, step, *refs):
    first = step == 1
    last = step == ITERS
    refs = list(refs)
    recv_ref, x_ref, stiff_ref, prof_ref = refs[:4]
    refs = refs[4:]
    if not last:
        w_ref = refs.pop(0)
    if first:
        pos_ref = refs.pop(0)
    else:
        sort_ref, pairs_ref, state_ref, v_ref, z_ref = refs[:5]
        refs = refs[5:]
    if first:
        sort_out, pairs_out = refs[:2]
        refs = refs[2:]
    send_ref, x_out, v_out, z_out, state_out, rows = refs
    x = x_ref[...]
    flat = comps * cil
    stiff = tall(column(stiff_ref[...], cil), comps)

    if first:
        pitch = PITCH[True]
        arrived = recv_ref[...]
        shape = (sources, sources * pitch)
        source, lane = lax.broadcasted_iota(jnp.int32, shape, 0), lane_iota(shape)
        chosen = jnp.where(lane == source * pitch + META, 1.0, 0.0).astype(BF16)
        meta = jnp.dot(chosen, arrived, preferred_element_type=F32)
        eye = lax.broadcasted_iota(jnp.int32, (sources, sources), 0) == lane_iota((sources, sources))
        named = [
            jnp.sum(jnp.where(eye, pick(meta, rank), 0.0), axis=0, keepdims=True) for rank in range(CAPD)
        ]
        named = jnp.concatenate(
            [jnp.broadcast_to(n, (TILE, sources)) for n in named], axis=0
        ).astype(BF16)

        def targets_for(pitch):
            shape = (sources, sources * pitch)
            source, lane = lax.broadcasted_iota(jnp.int32, shape, 0), lane_iota(shape)
            spread = jnp.where(lax.div(lane, pitch) == source, 1.0, 0.0).astype(BF16)
            wide = jnp.dot(named, spread, preferred_element_type=F32)
            return [wide[rank * TILE:rank * TILE + 1] for rank in range(CAPD)]

        sort_out[...] = sorting(comps, cil, sources, PITCH[False], targets_for(PITCH[False]))
        sort = sorting(comps, cil, sources, pitch, targets_for(pitch))
        rows[...] = jnp.dot(sort, arrived, preferred_element_type=F32)
        eps_three = 4.0 / total
        eps_two = eps_three ** (2.0 / 3.0)
        here = [
            jnp.broadcast_to(column(pos_ref[i:i + 1, :], cil), (cil, LANES)) for i in range(comps)
        ]
        start = flat + comps * sources + TILE
        for s in range(sources):
            gap = [
                here[i] - rows[start + i * sources + s:start + i * sources + s + 1]
                for i in range(comps)
            ]
            inverse = 1.0 / (gap[0] * gap[0] + gap[1] * gap[1] + gap[2] * gap[2] + eps_two)
            amplitude = eps_three * inverse * jnp.sqrt(inverse)
            slope = amplitude * inverse
            for (i, j), at in PAIRS.items():
                block = slope * gap[i] * gap[j]
                pairs_out[at, s] = block + amplitude if i == j else block
        pairs = lambda at, s: pairs_out[at, s]
    else:
        rows[...] = jnp.dot(sort_ref[...], recv_ref[...], preferred_element_type=F32)
        pairs = lambda at, s: pairs_ref[at, s]

    image, dots = applied(x, stiff, rows, pairs, prof_ref[...], comps, cil, sources)
    entries = {}
    if first:
        beta = jnp.sqrt(pick(dots, 0) + EPSILON)
        entries[BETA] = beta
        scale = 1.0 / beta
        basis = [x * scale]
        images = [image * scale]
    else:
        state = state_ref[...]
        count = step - 1
        gram, products, square = read_dots(dots, state, count)
        basis = [v_ref[j] for j in range(count)]
        images = [z_ref[j] for j in range(count)]
        heights, taken, length = heights_of(gram, products, square, shifts_of(count), count)
        scale = 1.0 / length
        vector, product = x, image
        for j in range(count):
            vector = vector - taken[j] * basis[j]
            product = product - taken[j] * images[j]
        basis.append(vector * scale)
        images.append(product * scale)
        for j in range(count):
            entries[GRAM[j, count - 1]] = gram[j, count - 1]
            entries[HESS[j, count - 1]] = heights[j]
        entries[HESS[count, count - 1]] = length
    row = pack(entries)
    state_out[...] = row if first else row + state
    for j in range(step):
        v_out[j] = basis[j]
        z_out[j] = images[j]
    outgoing = images[-1]
    for j, shift in enumerate(shifts_of(step)):
        if shift:
            outgoing = outgoing - shift * basis[j]
    pairs_of_dots = [(basis[j], basis[-1]) for j in range(step)]
    pairs_of_dots += [(basis[j], outgoing) for j in range(step)]
    pairs_of_dots.append((outgoing, outgoing))
    local = dot_row(pairs_of_dots)
    if last:
        to_every(send_ref, [local])
    else:
        to_every(send_ref, placed(outgoing, w_ref[...], place_of(cil), comps, cil) + [local])
    x_out[...] = outgoing


def shifts_of(count):
    if count == ITERS:
        return [0.0] * count
    return [0.0] * (count - 1) + [SHIFT]


def read_dots(dots, state, count):
    gram = {}
    for l in range(count):
        for j in range(l + 1):
            gram[j, l] = pick(dots, j) if l == count - 1 else pick(state, GRAM[j, l])
            gram[l, j] = gram[j, l]
    return gram, [pick(dots, count + j) for j in range(count)], pick(dots, 2 * count)


def heights_of(gram, products, square, shifts, count):
    heights, taken = [], []
    for j in range(count):
        extra = sum((shifts[l] * gram[j, l] for l in range(count) if shifts[l]), 0.0)
        heights.append(products[j] + extra)
        taken.append(heights[j] - shifts[j])
    norm = square
    for j in range(count):
        inner = -2.0 * products[j]
        for l in range(count):
            inner = inner + taken[l] * gram[j, l]
        norm = norm + taken[j] * inner
    return heights, taken, jnp.sqrt(jnp.maximum(norm, 0.0) + EPSILON)


def solve_kernel(rows_ref, state_ref, f_ref, v_ref, z_ref, solution_ref, residual_ref):
    dots = jnp.sum(rows_ref[...], axis=0)
    state = state_ref[...]
    gram, products, square = read_dots(dots, state, ITERS)
    heights, _, length = heights_of(gram, products, square, shifts_of(ITERS), ITERS)
    zero = jnp.zeros((1, 1), F32)
    columns = []
    for k in range(ITERS):
        if k == ITERS - 1:
            entries = heights + [length]
        else:
            entries = [pick(state, HESS[j, k]) for j in range(k + 2)]
        columns.append(entries + [zero] * (ITERS + 1 - len(entries)))
    units, triangle = [], {}
    for k in range(ITERS):
        vector = columns[k]
        for e in range(k):
            used = min(e + 2, k + 2)
            weight = sum(units[e][j] * vector[j] for j in range(used))
            triangle[e, k] = weight
            vector = [vector[j] - weight * units[e][j] if j < used else vector[j] for j in range(ITERS + 1)]
        size = jnp.sqrt(sum(vector[j] * vector[j] for j in range(k + 2)))
        triangle[k, k] = size
        units.append([vector[j] / size for j in range(ITERS + 1)])
    beta = pick(state, BETA)
    answers = [None] * ITERS
    for k in reversed(range(ITERS)):
        running = beta * units[k][0]
        for later in range(k + 1, ITERS):
            running = running - triangle[k, later] * answers[later]
        answers[k] = running / triangle[k, k]
    result = answers[0] * v_ref[0]
    rest = f_ref[...] - answers[0] * z_ref[0]
    for k in range(1, ITERS):
        result = result + answers[k] * v_ref[k]
        rest = rest - answers[k] * z_ref[k]
    solution_ref[...] = result
    residual_ref[...] = rest


def on_device(
    forcing,
    stiffness,
    positions,
    far_weights,
    far_profile,
    near_blocks,
    near_dest,
    near_cilia,
    near_count,
):
    rows = lax.axis_size("row")
    cols = lax.axis_size("col")
    comps, cil, points = forcing.shape
    slots = near_blocks.shape[0]
    width = comps * points
    flat = comps * cil
    total = cil * rows * cols
    chunk = 4
    struct = lambda *shape, dtype=F32: jax.ShapeDtypeStruct(shape, dtype)
    vmem, smem = pl.BlockSpec(memory_space=pltpu.VMEM), pl.BlockSpec(memory_space=pltpu.SMEM)
    slim = pltpu.CompilerParams(vmem_limit_bytes=4 << 20)
    roomy = pltpu.CompilerParams(vmem_limit_bytes=8 << 20)
    f = forcing.reshape(flat, points)
    stiff = stiffness.reshape(1, cil)
    weights = far_weights.reshape(1, points)
    profile = far_profile.reshape(1, points)
    cilia = near_cilia.T
    dest = near_dest.reshape(slots)

    blocks = pltpu.with_memory_space_constraint(near_blocks, pltpu.HBM)

    def exchange(send, x, first):
        arrived = lax.all_to_all(send, "row", split_axis=0, concat_axis=0, tiled=True)
        near = pl.pallas_call(
            functools.partial(near_kernel, comps, cil, chunk, first),
            out_shape=struct(cols, TILE, LANES, dtype=BF16),
            in_specs=[smem, smem, smem, vmem, pl.BlockSpec(memory_space=pltpu.HBM)],
            out_specs=vmem,
            scratch_shapes=[
                pltpu.VMEM((cil, TILE, width), BF16),
                pltpu.VMEM((cols, TILE, points), F32),
                pltpu.SMEM((cols,), jnp.int32),
                pltpu.VMEM(blocks.shape, BF16),
                pltpu.SemaphoreType.DMA((slots // chunk,)),
            ],
            compiler_params=pltpu.CompilerParams(vmem_limit_bytes=16 << 20),
            name="near",
        )(cilia, dest, near_count, x, blocks)
        out = pl.pallas_call(
            functools.partial(join_kernel, comps, first),
            out_shape=struct(cols, PITCH[first], LANES, dtype=BF16),
            compiler_params=slim,
            name="join",
        )(arrived, near)
        recv = lax.all_to_all(out, "col", split_axis=0, concat_axis=0, tiled=True)
        return recv.reshape(cols * PITCH[first], LANES)

    send = pl.pallas_call(
        functools.partial(first_kernel, comps, cil),
        out_shape=struct(rows, TILE, LANES),
        compiler_params=slim,
        name="first",
    )(f, positions, weights)
    recv = exchange(send, f, True)
    x = f
    sorted_rows = flat + comps * cols + TILE
    for step in range(1, ITERS + 1):
        first, last = step == 1, step == ITERS
        ins = [recv, x, stiff, profile]
        if not last:
            ins.append(weights)
        ins += [positions] if first else [sort, pairs, state, vs, zs]
        outs = []
        if first:
            outs += [
                struct(sorted_rows, cols * PITCH[False], dtype=BF16),
                struct(len(PAIRS), cols, cil, LANES),
            ]
        outs += [
            struct(rows * cols if last else rows, 1 if last else TILE, LANES),
            struct(flat, points),
            struct(step, flat, points),
            struct(step, flat, points),
            struct(1, LANES),
        ]
        results = pl.pallas_call(
            functools.partial(krylov_kernel, comps, cil, cols, total, step),
            out_shape=outs,
            scratch_shapes=[pltpu.VMEM((sorted_rows + comps * cols * first, LANES), F32)],
            compiler_params=roomy,
            name="krylov",
        )(*ins)
        if first:
            sort, pairs = results[:2]
            results = results[2:]
        send, x, vs, zs, state = results
        if not last:
            recv = exchange(send, x, False)
    everyone = lax.all_to_all(send, ("row", "col"), split_axis=0, concat_axis=0, tiled=True)
    out, rest = pl.pallas_call(
        solve_kernel, out_shape=[struct(flat, points)] * 2, compiler_params=slim, name="solve"
    )(everyone, state, f, vs, zs)
    return out.reshape(forcing.shape), rest.reshape(forcing.shape)


def solution(mesh):
    in_specs = (
        P(None, ("row", "col"), None),
        P(("row", "col")),
        P(None, ("row", "col")),
        P(),
        P(),
        P(("row", "col"), None, None),
        P(("row", "col"), None),
        P(("row", "col"), None),
        P(("row", "col")),
    )
    out_specs = (P(None, ("row", "col"), None), P(None, ("row", "col"), None))
    return jax.shard_map(
        on_device, mesh=mesh, in_specs=in_specs, out_specs=out_specs, check_vma=False
    )
```

```python
import functools
import jax
import jax.numpy as jnp
from jax import lax
from jax.experimental import pallas as pl
from jax.experimental.pallas import tpu as pltpu
from jax.sharding import PartitionSpec as P

CAPD = 2
ITERS = 4
EPSILON = 1e-06
F32 = jnp.float32
BF16 = jnp.bfloat16
HIGHEST = lax.Precision.HIGHEST
LANES = 128
GRAM = {(j, l): l * (l + 1) // 2 + j for l in range(ITERS) for j in range(l + 1)}
HESS = {(j, k): 16 + 8 * k + j for k in range(ITERS) for j in range(k + 2)}
BETA = 63
UPPER = {(e, k): 64 + 4 * k + e for k in range(ITERS) for e in range(k + 1)}
UNIT = {(k, j): 80 + 8 * k + j for k in range(ITERS) for j in range(k + 2)}
SHIFT = 2.0


def lane_iota(shape):
    return lax.broadcasted_iota(jnp.int32, shape, len(shape) - 1)


def column(row, size):
    eye = lax.broadcasted_iota(jnp.int32, (size, size), 0) == lane_iota((size, size))
    return jnp.sum(jnp.where(eye, row, 0.0), axis=1, keepdims=True)


def tall(col, comps):
    return jnp.concatenate([col] * comps, axis=0)


def bend(x, stiff):
    points = x.shape[1]
    lane = lane_iota(x.shape)

    def shifted(by):
        moved = pltpu.roll(x, by % points, 1)
        keep = lane >= by if by > 0 else lane < points + by
        return jnp.where(keep, moved, 0.0)

    fourth = shifted(2) - 4.0 * shifted(1) + 6.0 * x - 4.0 * shifted(-1) + shifted(-2)
    return x + stiff * fourth


def placed(x, weights, place, comps, cil):
    sums = jnp.sum(x * weights, axis=1, keepdims=True)
    return [
        jnp.sum(sums[i * cil:(i + 1) * cil] * place, axis=0, keepdims=True) for i in range(comps)
    ]


def place_of(cil):
    shape = (cil, LANES)
    own = lax.axis_index("row") * cil + lax.broadcasted_iota(jnp.int32, shape, 0)
    return jnp.where(lane_iota(shape) == own, 1.0, 0.0)


def to_every(send_ref, parts):
    if len(send_ref.shape) == 2:
        send_ref[...] = jnp.broadcast_to(parts[0], send_ref.shape)
        return
    rows = list(parts)
    rows += [jnp.zeros((1, LANES), F32)] * (send_ref.shape[1] - len(rows))
    tile = jnp.concatenate(rows, axis=0)
    send_ref[...] = jnp.broadcast_to(tile[None], send_ref.shape)


def dot_row(pairs):
    rows = [jnp.sum(a * b, axis=0, keepdims=True) for a, b in pairs]
    while len(rows) % 8:
        rows.append(jnp.zeros_like(rows[0]))
    sums = jnp.sum(jnp.concatenate(rows, axis=0), axis=1, keepdims=True)
    shape = (len(rows), LANES)
    eye = lax.broadcasted_iota(jnp.int32, shape, 0) == lane_iota(shape)
    return jnp.sum(jnp.where(eye, sums, 0.0), axis=0, keepdims=True)


def pick(row, lane):
    return row[:, lane:lane + 1]


def pack(entries):
    lane = lane_iota((1, LANES))
    row = jnp.zeros((1, LANES), F32)
    for where, value in entries.items():
        row = jnp.where(lane == where, value, row)
    return row


def first_kernel(comps, cil, f_hbm, pos_hbm, w_hbm, send_ref, x_out, pos_ref, w_ref, sems):
    copies = [
        pltpu.make_async_copy(source, target, sems.at[n])
        for n, (source, target) in enumerate(((f_hbm, x_out), (pos_hbm, pos_ref), (w_hbm, w_ref)))
    ]
    for copy in copies:
        copy.start()
    place = place_of(cil)
    for copy in copies:
        copy.wait()
    f = x_out[...]
    parts = placed(f, w_ref[...], place, comps, cil)
    parts.append(dot_row([(f, f)]))
    for i in range(comps):
        col = column(pos_ref[i:i + 1, :], cil)
        parts.append(jnp.sum(col * place, axis=0, keepdims=True))
    to_every(send_ref, parts)


TILE = 8
KEPT = 6
META = 6
DOTS = 14
PITCH = {True: 24, False: 16}


def near_kernel(comps, cil, chunk, first, cilia_hbm, dest_hbm, count_ref, x_ref, b_ref, kept_in, *refs):
    if first:
        out_ref, kept, lhs, result, used, held, cilia_ref, dest_ref, sems, table_sems = refs
    else:
        out_ref, lhs, result, used, held, cilia_ref, dest_ref, sems, table_sems = refs
        kept = kept_in
    points = x_ref.shape[1]
    slots = b_ref.shape[0]

    def block(slot):
        return kept[slot] if slot < KEPT else held[slot - KEPT]

    def fetches(at):
        start, stop = at * chunk, (at + 1) * chunk
        parts = []
        if first and start < KEPT:
            parts.append((start, min(stop, KEPT), kept, 0))
        if stop > KEPT:
            parts.append((max(start, KEPT), stop, held, KEPT))
        return [
            pltpu.make_async_copy(
                b_ref.at[pl.ds(begin, end - begin)],
                target.at[pl.ds(begin - offset, end - begin)],
                sems.at[at + (target is kept) * (slots // chunk)],
            )
            for begin, end, target, offset in parts
        ]


    tables = [
        pltpu.make_async_copy(source, target, table_sems.at[n])
        for n, (source, target) in enumerate(((cilia_hbm, cilia_ref), (dest_hbm, dest_ref)))
    ]
    for copy in tables:
        copy.start()
    for at in range(slots // chunk):
        for copy in fetches(at):
            copy.start()
    result[...] = jnp.zeros_like(result)

    def clear(i, carry):
        used[i] = 0
        return carry

    lax.fori_loop(0, used.shape[0], clear, 0)
    x = x_ref[...]
    high = x.astype(BF16).astype(F32)
    low = x - high
    row = lax.broadcasted_iota(jnp.int32, (TILE, points), 0)
    for g in range(cil):
        for i in range(comps):
            at = i * cil + g
            value = jnp.where(row == 0, high[at:at + 1], jnp.where(row == 1, low[at:at + 1], 0.0))
            lhs[g, :, i * points:(i + 1) * points] = value.astype(BF16)
    lane = lane_iota((1, points))
    for copy in tables:
        copy.wait()
    for at in range(slots // chunk):
        for copy in fetches(at):
            copy.wait()
        speeds = [
            lax.dot_general(
                lhs[cilia_ref[0, slot]], block(slot), (((1,), (1,)), ((), ())),
                preferred_element_type=F32,
            )
            for slot in range(at * chunk, (at + 1) * chunk)
        ]
        for s in range(chunk):
            slot = at * chunk + s
            dest = dest_ref[slot]
            rank = used[dest]
            used[dest] = rank + 1
            live = slot < count_ref[0]
            speed = jnp.where(live, speeds[s][0:1] + speeds[s][1:2], 0.0)
            for i in range(comps):
                result[dest, pl.ds(rank * comps + i, 1), :] = speed[:, i * points:(i + 1) * points]
            if first:
                target = cilia_ref[1, slot].astype(F32)
                before = result[dest, META:META + 1, :]
                result[dest, META:META + 1, :] = jnp.where(lane == rank, target, before)
    out_ref[...] = result[...].astype(BF16)


def join_kernel(comps, first, rows_ref, near_ref, send_ref):
    total = jnp.sum(rows_ref[...], axis=0)
    high = total.astype(BF16).astype(F32)
    rest = total - high
    middle = rest.astype(BF16).astype(F32)
    low = rest - middle
    at = comps
    shared = jnp.concatenate(
        [
            high[:at], rest[:at], high[at:at + 1],
            middle[at:at + 1] + pltpu.roll(low[at:at + 1], LANES // 2, 1),
        ],
        axis=0,
    )
    send_ref[:, :TILE, :] = near_ref[...]
    send_ref[:, TILE:2 * TILE, :] = jnp.broadcast_to(
        shared.astype(BF16)[None], (send_ref.shape[0],) + shared.shape
    )
    if first:
        at = comps + 1
        places = jnp.concatenate(
            [high[at:at + comps], rest[at:at + comps], jnp.zeros((TILE - 2 * comps, LANES), F32)], axis=0
        )
        send_ref[:, 2 * TILE:3 * TILE, :] = jnp.broadcast_to(
            places.astype(BF16)[None], (send_ref.shape[0],) + places.shape
        )


def sorting(comps, cil, sources, pitch, targets):
    def parts(rows):
        shape = (rows, sources * pitch)
        row = lax.broadcasted_iota(jnp.int32, shape, 0)
        lane = lane_iota(shape)
        return row, lax.div(lane, pitch), lax.rem(lane, pitch)

    row, _, place = parts(comps * cil)
    comp, cilium = lax.div(row, cil), lax.rem(row, cil).astype(F32)
    found = jnp.zeros(row.shape, jnp.bool_)
    for rank in range(CAPD):
        found |= (place == rank * comps + comp) & (cilium == targets[rank])
    pieces = [found]

    def gathered(start):
        row, source, place = parts(comps * sources)
        comp, wanted = lax.div(row, sources), lax.rem(row, sources)
        here = (place == start + comp) | (place == start + comps + comp)
        return here & (source == wanted)

    pieces.append(gathered(TILE))
    row, _, place = parts(TILE)
    pieces.append((row == 0) & ((place == DOTS) | (place == DOTS + 1)))
    if pitch > 2 * TILE:
        pieces.append(gathered(2 * TILE))
    return jnp.concatenate([jnp.where(p, 1.0, 0.0) for p in pieces], axis=0).astype(BF16)


def applied(x, stiff, rows, pairs, profile, comps, cil, sources):
    flat = comps * cil
    image = bend(x, stiff) + rows[:flat]
    totals = [jnp.zeros((cil, LANES), F32) for _ in range(comps)]
    for s in range(sources):
        strength = [rows[flat + j * sources + s:flat + j * sources + s + 1] for j in range(comps)]
        along = [pairs(1 + j, s) for j in range(comps)]
        projected = sum(along[j] * strength[j] for j in range(comps))
        direct = pairs(0, s)
        for i in range(comps):
            totals[i] = totals[i] + (direct * strength[i] + along[i] * projected)
    far = jnp.concatenate([jnp.sum(t, axis=1, keepdims=True) for t in totals], axis=0)
    dots = rows[flat + comps * sources:flat + comps * sources + 1]
    dots = dots + pltpu.roll(dots, LANES // 2, 1)
    return image + far * profile, dots


def krylov_kernel(comps, cil, sources, total, step, *refs):
    first = step == 1
    last = step == ITERS
    refs = list(refs)
    recv_ref, x_ref, stiff_ref, prof_ref = refs[:4]
    refs = refs[4:]
    if not last:
        w_ref = refs.pop(0)
    if first:
        pos_ref = refs.pop(0)
    else:
        sort_ref, pairs_ref, state_ref, v_ref, z_ref = refs[:5]
        refs = refs[5:]
    if first:
        sort_out, pairs_out = refs[:2]
        refs = refs[2:]
    send_ref, x_out, v_out, z_out, state_out, rows = refs
    x = x_ref[...]
    flat = comps * cil
    stiff = tall(column(stiff_ref[...], cil), comps)

    if first:
        pitch = PITCH[True]
        arrived = recv_ref[...]
        shape = (sources, sources * pitch)
        source, lane = lax.broadcasted_iota(jnp.int32, shape, 0), lane_iota(shape)
        chosen = jnp.where(lane == source * pitch + META, 1.0, 0.0).astype(BF16)
        meta = jnp.dot(chosen, arrived, preferred_element_type=F32)
        eye = lax.broadcasted_iota(jnp.int32, (sources, sources), 0) == lane_iota((sources, sources))
        named = [
            jnp.sum(jnp.where(eye, pick(meta, rank), 0.0), axis=0, keepdims=True) for rank in range(CAPD)
        ]
        named = jnp.concatenate(
            [jnp.broadcast_to(n, (TILE, sources)) for n in named], axis=0
        ).astype(BF16)

        def targets_for(pitch):
            shape = (sources, sources * pitch)
            source, lane = lax.broadcasted_iota(jnp.int32, shape, 0), lane_iota(shape)
            spread = jnp.where(lax.div(lane, pitch) == source, 1.0, 0.0).astype(BF16)
            wide = jnp.dot(named, spread, preferred_element_type=F32)
            return [wide[rank * TILE:rank * TILE + 1] for rank in range(CAPD)]

        sort_out[...] = sorting(comps, cil, sources, PITCH[False], targets_for(PITCH[False]))
        sort = sorting(comps, cil, sources, pitch, targets_for(pitch))
        rows[...] = jnp.dot(sort, arrived, preferred_element_type=F32)
        eps_three = 4.0 / total
        eps_two = eps_three ** (2.0 / 3.0)
        here = [
            jnp.broadcast_to(column(pos_ref[i:i + 1, :], cil), (cil, LANES)) for i in range(comps)
        ]
        start = flat + comps * sources + TILE
        for s in range(sources):
            gap = [
                here[i] - rows[start + i * sources + s:start + i * sources + s + 1]
                for i in range(comps)
            ]
            inverse = 1.0 / (gap[0] * gap[0] + gap[1] * gap[1] + gap[2] * gap[2] + eps_two)
            amplitude = eps_three * inverse * jnp.sqrt(inverse)
            slope = jnp.sqrt(amplitude * inverse)
            pairs_out[0, s] = amplitude
            for i in range(comps):
                pairs_out[1 + i, s] = slope * gap[i]
        pairs = lambda at, s: pairs_out[at, s]
    else:
        rows[...] = jnp.dot(sort_ref[...], recv_ref[...], preferred_element_type=F32)
        pairs = lambda at, s: pairs_ref[at, s]

    image, dots = applied(x, stiff, rows, pairs, prof_ref[...], comps, cil, sources)
    entries = {}
    if first:
        beta = jnp.sqrt(pick(dots, 0) + EPSILON)
        entries[BETA] = beta
        scale = 1.0 / beta
        basis = [x * scale]
        images = [image * scale]
    else:
        state = state_ref[...]
        count = step - 1
        gram, products, square = read_dots(dots, state, count)
        basis = [v_ref[j] for j in range(count)]
        images = [z_ref[j] for j in range(count)]
        heights, taken, length = heights_of(gram, products, square, shifts_of(count), count)
        scale = 1.0 / length
        vector, product = x, image
        for j in range(count):
            vector = vector - taken[j] * basis[j]
            product = product - taken[j] * images[j]
        basis.append(vector * scale)
        images.append(product * scale)
        for j in range(count):
            entries[GRAM[j, count - 1]] = gram[j, count - 1]
            entries[HESS[j, count - 1]] = heights[j]
        entries[HESS[count, count - 1]] = length
        if last:
            units = []
            for k in range(count - 1):
                vector = [pick(state, HESS[j, k]) for j in range(k + 2)]
                weights, unit = orthogonalized(vector, units, k + 2)
                units.append(unit)
                entries.update({UPPER[e, k]: weights[e] for e in range(k + 1)})
                entries.update({UNIT[k, j]: unit[j] for j in range(k + 2)})
    row = pack(entries)
    state_out[...] = row if first else row + state
    for j in range(step):
        v_out[j] = basis[j]
        z_out[j] = images[j]
    outgoing = images[-1]
    for j, shift in enumerate(shifts_of(step)):
        if shift:
            outgoing = outgoing - shift * basis[j]
    pairs_of_dots = [(basis[j], basis[-1]) for j in range(step)]
    pairs_of_dots += [(basis[j], outgoing) for j in range(step)]
    pairs_of_dots.append((outgoing, outgoing))
    local = dot_row(pairs_of_dots)
    if last:
        to_every(send_ref, [local])
    else:
        to_every(send_ref, placed(outgoing, w_ref[...], place_of(cil), comps, cil) + [local])
    x_out[...] = outgoing


def shifts_of(count):
    if count == ITERS:
        return [0.0] * count
    return [0.0] * (count - 1) + [SHIFT]


def read_dots(dots, state, count):
    gram = {}
    for l in range(count):
        for j in range(l + 1):
            gram[j, l] = pick(dots, j) if l == count - 1 else pick(state, GRAM[j, l])
            gram[l, j] = gram[j, l]
    return gram, [pick(dots, count + j) for j in range(count)], pick(dots, 2 * count)


def heights_of(gram, products, square, shifts, count):
    heights, taken = [], []
    for j in range(count):
        extra = sum((shifts[l] * gram[j, l] for l in range(count) if shifts[l]), 0.0)
        heights.append(products[j] + extra)
        taken.append(heights[j] - shifts[j])
    norm = square
    for j in range(count):
        inner = -2.0 * products[j]
        for l in range(count):
            inner = inner + taken[l] * gram[j, l]
        norm = norm + taken[j] * inner
    return heights, taken, jnp.sqrt(jnp.maximum(norm, 0.0) + EPSILON)


def orthogonalized(vector, units, length):
    weights = []
    for e, unit in enumerate(units):
        used = min(e + 2, length)
        weight = sum(unit[j] * vector[j] for j in range(used))
        weights.append(weight)
        vector = [vector[j] - weight * unit[j] if j < used else vector[j] for j in range(length)]
    square = sum(entry * entry for entry in vector)
    size = jnp.sqrt(square)
    weights.append(size)
    return weights, [entry / size for entry in vector]


def solve_kernel(rows_ref, state_ref, f_ref, v_ref, z_ref, solution_ref, residual_ref):
    state = state_ref[...]
    known = ITERS - 2
    units = [[pick(state, UNIT[k, j]) for j in range(k + 2)] for k in range(known)]
    triangle = {(e, k): pick(state, UPPER[e, k]) for k in range(known) for e in range(k + 1)}
    beta = pick(state, BETA)
    dots = jnp.sum(rows_ref[...], axis=0, keepdims=True)
    gram, products, square = read_dots(dots, state, ITERS)
    heights, _, length = heights_of(gram, products, square, shifts_of(ITERS), ITERS)
    for k in range(known, ITERS):
        if k == ITERS - 1:
            vector = heights + [length]
        else:
            vector = [pick(state, HESS[j, k]) for j in range(k + 2)]
        weights, unit = orthogonalized(vector, units, k + 2)
        units.append(unit)
        triangle.update({(e, k): weights[e] for e in range(k + 1)})
    answers = [None] * ITERS
    for k in reversed(range(ITERS)):
        running = beta * units[k][0]
        for later in reversed(range(k + 1, ITERS)):
            running = running - triangle[k, later] * answers[later]
        answers[k] = running / triangle[k, k]
    result = answers[0] * v_ref[0]
    rest = f_ref[...] - answers[0] * z_ref[0]
    for k in range(1, ITERS):
        result = result + answers[k] * v_ref[k]
        rest = rest - answers[k] * z_ref[k]
    solution_ref[...] = result
    residual_ref[...] = rest


def on_device(
    forcing,
    stiffness,
    positions,
    far_weights,
    far_profile,
    near_blocks,
    near_dest,
    near_cilia,
    near_count,
):
    rows = lax.axis_size("row")
    cols = lax.axis_size("col")
    comps, cil, points = forcing.shape
    slots = near_blocks.shape[0]
    width = comps * points
    flat = comps * cil
    total = cil * rows * cols
    chunk = 4
    struct = lambda *shape, dtype=F32: jax.ShapeDtypeStruct(shape, dtype)
    vmem, smem, hbm = (pl.BlockSpec(memory_space=m) for m in (pltpu.VMEM, pltpu.SMEM, pltpu.HBM))
    slim = pltpu.CompilerParams(vmem_limit_bytes=4 << 20)
    roomy = pltpu.CompilerParams(vmem_limit_bytes=8 << 20)
    f = forcing.reshape(flat, points)
    stiff = stiffness.reshape(1, cil)
    weights = far_weights.reshape(1, points)
    profile = far_profile.reshape(1, points)
    in_hbm = lambda array: pltpu.with_memory_space_constraint(array, pltpu.HBM)
    blocks = in_hbm(near_blocks)
    cilia = in_hbm(near_cilia.T)
    dest = in_hbm(near_dest.reshape(slots))


    def exchange(send, x, kept, first):
        arrived = lax.all_to_all(send, "row", split_axis=0, concat_axis=0, tiled=True)
        outs = [struct(cols, TILE, LANES, dtype=BF16)]
        if first:
            outs.append(pltpu.VMEM((KEPT, width, width), BF16))
        near, *fetched = pl.pallas_call(
            functools.partial(near_kernel, comps, cil, chunk, first),
            out_shape=outs,
            in_specs=[hbm, hbm, smem, vmem, hbm, smem if first else vmem],
            out_specs=[vmem] * len(outs),
            scratch_shapes=[
                pltpu.VMEM((cil, TILE, width), BF16),
                pltpu.VMEM((cols, TILE, points), F32),
                pltpu.SMEM((cols,), jnp.int32),
                pltpu.VMEM((slots - KEPT, width, width), BF16),
                pltpu.SMEM(cilia.shape, jnp.int32),
                pltpu.SMEM(dest.shape, jnp.int32),
                pltpu.SemaphoreType.DMA((2 * slots // chunk,)),
                pltpu.SemaphoreType.DMA((2,)),
            ],
            compiler_params=pltpu.CompilerParams(vmem_limit_bytes=16 << 20),
            name="near",
        )(cilia, dest, near_count, x, blocks, near_count if first else kept)
        out = pl.pallas_call(
            functools.partial(join_kernel, comps, first),
            out_shape=struct(cols, PITCH[first], LANES, dtype=BF16),
            compiler_params=slim,
            name="join",
        )(arrived, near)
        recv = lax.all_to_all(out, "col", split_axis=0, concat_axis=0, tiled=True)
        return recv.reshape(cols * PITCH[first], LANES), fetched[0] if first else kept

    send, x = pl.pallas_call(
        functools.partial(first_kernel, comps, cil),
        out_shape=[struct(rows, TILE, LANES), struct(flat, points)],
        in_specs=[hbm, hbm, hbm],
        out_specs=[vmem, vmem],
        scratch_shapes=[
            pltpu.VMEM((comps, cil), F32),
            pltpu.VMEM((1, points), F32),
            pltpu.SemaphoreType.DMA((comps,)),
        ],
        compiler_params=slim,
        name="first",
    )(in_hbm(f), in_hbm(positions), in_hbm(weights))
    recv, kept = exchange(send, x, None, True)
    sorted_rows = flat + comps * cols + TILE
    for step in range(1, ITERS + 1):
        first, last = step == 1, step == ITERS
        ins = [recv, x, stiff, profile]
        if not last:
            ins.append(weights)
        ins += [positions] if first else [sort, pairs, state, vs, zs]
        outs = []
        if first:
            outs += [
                struct(sorted_rows, cols * PITCH[False], dtype=BF16),
                struct(1 + comps, cols, cil, LANES),
            ]
        outs += [
            struct(rows * cols, LANES) if last else struct(rows, TILE, LANES),
            struct(flat, points),
            struct(step, flat, points),
            struct(step, flat, points),
            struct(1, LANES),
        ]
        results = pl.pallas_call(
            functools.partial(krylov_kernel, comps, cil, cols, total, step),
            out_shape=outs,
            scratch_shapes=[pltpu.VMEM((sorted_rows + comps * cols * first, LANES), F32)],
            compiler_params=roomy,
            name="krylov",
        )(*ins)
        if first:
            sort, pairs = results[:2]
            results = results[2:]
        send, x, vs, zs, state = results
        if not last:
            recv, _ = exchange(send, x, kept, False)
    everyone = lax.all_to_all(send, ("row", "col"), split_axis=0, concat_axis=0, tiled=True)
    out, rest = pl.pallas_call(
        solve_kernel, out_shape=[struct(flat, points)] * 2, compiler_params=slim, name="solve"
    )(everyone, state, f, vs, zs)
    return out.reshape(forcing.shape), rest.reshape(forcing.shape)


def solution(mesh):
    in_specs = (
        P(None, ("row", "col"), None),
        P(("row", "col")),
        P(None, ("row", "col")),
        P(),
        P(),
        P(("row", "col"), None, None),
        P(("row", "col"), None),
        P(("row", "col"), None),
        P(("row", "col")),
    )
    out_specs = (P(None, ("row", "col"), None), P(None, ("row", "col"), None))
    return jax.shard_map(
        on_device, mesh=mesh, in_specs=in_specs, out_specs=out_specs, check_vma=False
    )
```

```python
import functools
import jax
import jax.numpy as jnp
from jax import lax
from jax.experimental import pallas as pl
from jax.experimental.pallas import tpu as pltpu
from jax.sharding import PartitionSpec as P

CAPD = 2
ITERS = 4
EPSILON = 1e-06
F32 = jnp.float32
BF16 = jnp.bfloat16
HIGHEST = lax.Precision.HIGHEST
LANES = 128
GRAM = {(j, l): l * (l + 1) // 2 + j for l in range(ITERS) for j in range(l + 1)}
HESS = {(j, k): 16 + 8 * k + j for k in range(ITERS) for j in range(k + 2)}
BETA = 63
UPPER = {(e, k): 64 + 4 * k + e for k in range(ITERS) for e in range(k + 1)}
UNIT = {(k, j): 80 + 8 * k + j for k in range(ITERS) for j in range(k + 2)}
SHIFT = 2.0


def lane_iota(shape):
    return lax.broadcasted_iota(jnp.int32, shape, len(shape) - 1)


def column(row, size):
    eye = lax.broadcasted_iota(jnp.int32, (size, size), 0) == lane_iota((size, size))
    return jnp.sum(jnp.where(eye, row, 0.0), axis=1, keepdims=True)


def tall(col, comps):
    return jnp.concatenate([col] * comps, axis=0)


def bend(x, stiff):
    points = x.shape[1]
    lane = lane_iota(x.shape)

    def shifted(by):
        moved = pltpu.roll(x, by % points, 1)
        keep = lane >= by if by > 0 else lane < points + by
        return jnp.where(keep, moved, 0.0)

    fourth = shifted(2) - 4.0 * shifted(1) + 6.0 * x - 4.0 * shifted(-1) + shifted(-2)
    return x + stiff * fourth


def placed(x, weights, place, comps, cil):
    sums = jnp.sum(x * weights, axis=1, keepdims=True)
    return [
        jnp.sum(sums[i * cil:(i + 1) * cil] * place, axis=0, keepdims=True) for i in range(comps)
    ]


def place_of(cil):
    shape = (cil, LANES)
    own = lax.axis_index("row") * cil + lax.broadcasted_iota(jnp.int32, shape, 0)
    return jnp.where(lane_iota(shape) == own, 1.0, 0.0)


def to_every(send_ref, parts):
    if len(send_ref.shape) == 2:
        send_ref[...] = jnp.broadcast_to(parts[0], send_ref.shape)
        return
    rows = list(parts)
    rows += [jnp.zeros((1, LANES), F32)] * (send_ref.shape[1] - len(rows))
    tile = jnp.concatenate(rows, axis=0)
    send_ref[...] = jnp.broadcast_to(tile[None], send_ref.shape)


def dot_row(pairs):
    rows = [jnp.sum(a * b, axis=0, keepdims=True) for a, b in pairs]
    while len(rows) % 8:
        rows.append(jnp.zeros_like(rows[0]))
    sums = jnp.sum(jnp.concatenate(rows, axis=0), axis=1, keepdims=True)
    shape = (len(rows), LANES)
    eye = lax.broadcasted_iota(jnp.int32, shape, 0) == lane_iota(shape)
    return jnp.sum(jnp.where(eye, sums, 0.0), axis=0, keepdims=True)


def pick(row, lane):
    return row[:, lane:lane + 1]


def pack(entries):
    lane = lane_iota((1, LANES))
    row = jnp.zeros((1, LANES), F32)
    for where, value in entries.items():
        row = jnp.where(lane == where, value, row)
    return row


def first_kernel(comps, cil, f_hbm, pos_hbm, w_hbm, send_ref, x_out, pos_ref, w_ref, sems):
    copies = [
        pltpu.make_async_copy(source, target, sems.at[n])
        for n, (source, target) in enumerate(((f_hbm, x_out), (pos_hbm, pos_ref), (w_hbm, w_ref)))
    ]
    for copy in copies:
        copy.start()
    place = place_of(cil)
    for copy in copies:
        copy.wait()
    f = x_out[...]
    parts = placed(f, w_ref[...], place, comps, cil)
    parts.append(dot_row([(f, f)]))
    for i in range(comps):
        col = column(pos_ref[i:i + 1, :], cil)
        parts.append(jnp.sum(col * place, axis=0, keepdims=True))
    to_every(send_ref, parts)


TILE = 8
KEPT = 6
CHUNKS = (8, 8, 8, 8)
META = 6
DOTS = 14
PITCH = {True: 24, False: 16}


def near_kernel(comps, cil, first, cilia_hbm, table_hbm, count_ref, x_ref, b_ref, *refs):
    refs = list(refs)
    if not first:
        kept = refs.pop(0)
    out_ref = refs.pop(0)
    if first:
        kept, place_ref = refs[:2]
        refs = refs[2:]
    lhs, result, used, held, cilia_ref, table_ref, sems, table_sems = refs
    points = x_ref.shape[1]
    slots = b_ref.shape[0]
    bounds = [(sum(CHUNKS[:n]), sum(CHUNKS[:n + 1])) for n in range(len(CHUNKS))]

    def block(slot):
        return kept[slot] if slot < KEPT else held[slot - KEPT]

    def fetches(n):
        start, stop = bounds[n]
        parts = []
        if first and start < KEPT:
            parts.append((start, min(stop, KEPT), kept, 0))
        if stop > KEPT:
            parts.append((max(start, KEPT), stop, held, KEPT))
        return [
            pltpu.make_async_copy(
                b_ref.at[pl.ds(begin, end - begin)],
                target.at[pl.ds(begin - offset, end - begin)],
                sems.at[n + (target is kept) * len(CHUNKS)],
            )
            for begin, end, target, offset in parts
        ]

    tables = [
        pltpu.make_async_copy(source, target, table_sems.at[n])
        for n, (source, target) in enumerate(((cilia_hbm, cilia_ref), (table_hbm, table_ref)))
    ]
    for copy in tables:
        copy.start()
    for n in range(len(CHUNKS)):
        for copy in fetches(n):
            copy.start()
    result[...] = jnp.zeros_like(result)
    x = x_ref[...]
    high = x.astype(BF16).astype(F32)
    low = x - high
    row = lax.broadcasted_iota(jnp.int32, (TILE, points), 0)
    for g in range(cil):
        for i in range(comps):
            at = i * cil + g
            value = jnp.where(row == 0, high[at:at + 1], jnp.where(row == 1, low[at:at + 1], 0.0))
            lhs[g, :, i * points:(i + 1) * points] = value.astype(BF16)
    for copy in tables:
        copy.wait()
    if first:
        lane = lane_iota((1, points))
        for dest in range(used.shape[0]):
            used[dest] = 0
        for slot in range(slots):
            dest = table_ref[slot]
            rank = used[dest]
            used[dest] = rank + 1
            place_ref[slot] = dest * TILE + rank * comps
            at = pl.ds(dest * TILE + META, 1)
            target = cilia_ref[1, slot].astype(F32)
            result[at, :] = jnp.where(lane == rank, target, result[at, :])
    else:
        place_ref = table_ref
    for n, (start, stop) in enumerate(bounds):
        for copy in fetches(n):
            copy.wait()
        speeds = [
            lax.dot_general(
                lhs[cilia_ref[0, slot]], block(slot), (((1,), (1,)), ((), ())),
                preferred_element_type=F32,
            )
            for slot in range(start, stop)
        ]
        for slot, speed in zip(range(start, stop), speeds):
            speed = jnp.where(slot < count_ref[0], speed[0:1] + speed[1:2], 0.0)
            for i in range(comps):
                result[pl.ds(place_ref[slot] + i, 1), :] = speed[:, i * points:(i + 1) * points]
    out_ref[...] = result[...].astype(BF16).reshape(out_ref.shape)


def join_kernel(comps, first, rows_ref, near_ref, send_ref):
    total = jnp.sum(rows_ref[...], axis=0)
    high = total.astype(BF16).astype(F32)
    rest = total - high
    middle = rest.astype(BF16).astype(F32)
    low = rest - middle
    at = comps
    shared = jnp.concatenate(
        [
            high[:at], rest[:at], high[at:at + 1],
            middle[at:at + 1] + pltpu.roll(low[at:at + 1], LANES // 2, 1),
        ],
        axis=0,
    )
    send_ref[:, :TILE, :] = near_ref[...]
    send_ref[:, TILE:2 * TILE, :] = jnp.broadcast_to(
        shared.astype(BF16)[None], (send_ref.shape[0],) + shared.shape
    )
    if first:
        at = comps + 1
        places = jnp.concatenate(
            [high[at:at + comps], rest[at:at + comps], jnp.zeros((TILE - 2 * comps, LANES), F32)], axis=0
        )
        send_ref[:, 2 * TILE:3 * TILE, :] = jnp.broadcast_to(
            places.astype(BF16)[None], (send_ref.shape[0],) + places.shape
        )


def sorting(comps, cil, sources, pitch, targets):
    def parts(rows):
        shape = (rows, sources * pitch)
        row = lax.broadcasted_iota(jnp.int32, shape, 0)
        lane = lane_iota(shape)
        return row, lax.div(lane, pitch), lax.rem(lane, pitch)

    row, _, place = parts(comps * cil)
    comp, cilium = lax.div(row, cil), lax.rem(row, cil).astype(F32)
    found = jnp.zeros(row.shape, jnp.bool_)
    for rank in range(CAPD):
        found |= (place == rank * comps + comp) & (cilium == targets[rank])
    pieces = [found]

    def gathered(start):
        row, source, place = parts(comps * sources)
        comp, wanted = lax.div(row, sources), lax.rem(row, sources)
        here = (place == start + comp) | (place == start + comps + comp)
        return here & (source == wanted)

    pieces.append(gathered(TILE))
    row, _, place = parts(TILE)
    pieces.append((row == 0) & ((place == DOTS) | (place == DOTS + 1)))
    if pitch > 2 * TILE:
        pieces.append(gathered(2 * TILE))
    return jnp.concatenate([jnp.where(p, 1.0, 0.0) for p in pieces], axis=0).astype(BF16)


def applied(x, stiff, rows, pairs, profile, comps, cil, sources):
    flat = comps * cil
    image = bend(x, stiff) + rows[:flat]
    totals = [jnp.zeros((cil, LANES), F32) for _ in range(comps)]
    for s in range(sources):
        strength = [rows[flat + j * sources + s:flat + j * sources + s + 1] for j in range(comps)]
        along = [pairs(1 + j, s) for j in range(comps)]
        projected = sum(along[j] * strength[j] for j in range(comps))
        direct = pairs(0, s)
        for i in range(comps):
            totals[i] = totals[i] + (direct * strength[i] + along[i] * projected)
    far = jnp.concatenate([jnp.sum(t, axis=1, keepdims=True) for t in totals], axis=0)
    dots = rows[flat + comps * sources:flat + comps * sources + 1]
    dots = dots + pltpu.roll(dots, LANES // 2, 1)
    return image + far * profile, dots


def krylov_kernel(comps, cil, sources, total, step, *refs):
    first = step == 1
    last = step == ITERS
    refs = list(refs)
    recv_ref, x_ref, stiff_ref, prof_ref = refs[:4]
    refs = refs[4:]
    if not last:
        w_ref = refs.pop(0)
    if first:
        pos_ref = refs.pop(0)
    else:
        sort_ref, pairs_ref, state_ref, v_ref, z_ref = refs[:5]
        refs = refs[5:]
    if first:
        sort_out, pairs_out = refs[:2]
        refs = refs[2:]
    send_ref, x_out, v_out, z_out, state_out, rows = refs
    x = x_ref[...]
    flat = comps * cil
    stiff = tall(column(stiff_ref[...], cil), comps)

    if first:
        pitch = PITCH[True]
        arrived = recv_ref[...]
        shape = (sources, sources * pitch)
        source, lane = lax.broadcasted_iota(jnp.int32, shape, 0), lane_iota(shape)
        chosen = jnp.where(lane == source * pitch + META, 1.0, 0.0).astype(BF16)
        meta = jnp.dot(chosen, arrived, preferred_element_type=F32)
        eye = lax.broadcasted_iota(jnp.int32, (sources, sources), 0) == lane_iota((sources, sources))
        named = [
            jnp.sum(jnp.where(eye, pick(meta, rank), 0.0), axis=0, keepdims=True) for rank in range(CAPD)
        ]
        named = jnp.concatenate(
            [jnp.broadcast_to(n, (TILE, sources)) for n in named], axis=0
        ).astype(BF16)

        def targets_for(pitch):
            shape = (sources, sources * pitch)
            source, lane = lax.broadcasted_iota(jnp.int32, shape, 0), lane_iota(shape)
            spread = jnp.where(lax.div(lane, pitch) == source, 1.0, 0.0).astype(BF16)
            wide = jnp.dot(named, spread, preferred_element_type=F32)
            return [wide[rank * TILE:rank * TILE + 1] for rank in range(CAPD)]

        sort_out[...] = sorting(comps, cil, sources, PITCH[False], targets_for(PITCH[False]))
        sort = sorting(comps, cil, sources, pitch, targets_for(pitch))
        rows[...] = jnp.dot(sort, arrived, preferred_element_type=F32)
        eps_three = 4.0 / total
        eps_two = eps_three ** (2.0 / 3.0)
        here = [
            jnp.broadcast_to(column(pos_ref[i:i + 1, :], cil), (cil, LANES)) for i in range(comps)
        ]
        start = flat + comps * sources + TILE
        for s in range(sources):
            gap = [
                here[i] - rows[start + i * sources + s:start + i * sources + s + 1]
                for i in range(comps)
            ]
            inverse = 1.0 / (gap[0] * gap[0] + gap[1] * gap[1] + gap[2] * gap[2] + eps_two)
            amplitude = eps_three * inverse * jnp.sqrt(inverse)
            slope = jnp.sqrt(amplitude * inverse)
            pairs_out[0, s] = amplitude
            for i in range(comps):
                pairs_out[1 + i, s] = slope * gap[i]
        pairs = lambda at, s: pairs_out[at, s]
    else:
        rows[...] = jnp.dot(sort_ref[...], recv_ref[...], preferred_element_type=F32)
        pairs = lambda at, s: pairs_ref[at, s]

    image, dots = applied(x, stiff, rows, pairs, prof_ref[...], comps, cil, sources)
    entries = {}
    if first:
        beta = jnp.sqrt(pick(dots, 0) + EPSILON)
        entries[BETA] = beta
        scale = 1.0 / beta
        basis = [x * scale]
        images = [image * scale]
    else:
        state = state_ref[...]
        count = step - 1
        gram, products, square = read_dots(dots, state, count)
        basis = [v_ref[j] for j in range(count)]
        images = [z_ref[j] for j in range(count)]
        heights, taken, length = heights_of(gram, products, square, shifts_of(count), count)
        scale = 1.0 / length
        vector, product = x, image
        for j in range(count):
            vector = vector - taken[j] * basis[j]
            product = product - taken[j] * images[j]
        basis.append(vector * scale)
        images.append(product * scale)
        for j in range(count):
            entries[GRAM[j, count - 1]] = gram[j, count - 1]
            entries[HESS[j, count - 1]] = heights[j]
        entries[HESS[count, count - 1]] = length
        if last:
            units = []
            for k in range(count - 1):
                vector = [pick(state, HESS[j, k]) for j in range(k + 2)]
                weights, unit = orthogonalized(vector, units, k + 2)
                units.append(unit)
                entries.update({UPPER[e, k]: weights[e] for e in range(k + 1)})
                entries.update({UNIT[k, j]: unit[j] for j in range(k + 2)})
    row = pack(entries)
    state_out[...] = row if first else row + state
    for j in range(step):
        v_out[j] = basis[j]
        z_out[j] = images[j]
    outgoing = images[-1]
    for j, shift in enumerate(shifts_of(step)):
        if shift:
            outgoing = outgoing - shift * basis[j]
    pairs_of_dots = [(basis[j], basis[-1]) for j in range(step)]
    pairs_of_dots += [(basis[j], outgoing) for j in range(step)]
    pairs_of_dots.append((outgoing, outgoing))
    local = dot_row(pairs_of_dots)
    if last:
        to_every(send_ref, [local])
    else:
        to_every(send_ref, placed(outgoing, w_ref[...], place_of(cil), comps, cil) + [local])
    x_out[...] = outgoing


def shifts_of(count):
    if count == ITERS:
        return [0.0] * count
    return [0.0] * (count - 1) + [SHIFT]


def read_dots(dots, state, count):
    gram = {}
    for l in range(count):
        for j in range(l + 1):
            gram[j, l] = pick(dots, j) if l == count - 1 else pick(state, GRAM[j, l])
            gram[l, j] = gram[j, l]
    return gram, [pick(dots, count + j) for j in range(count)], pick(dots, 2 * count)


def heights_of(gram, products, square, shifts, count):
    heights, taken = [], []
    for j in range(count):
        extra = sum((shifts[l] * gram[j, l] for l in range(count) if shifts[l]), 0.0)
        heights.append(products[j] + extra)
        taken.append(heights[j] - shifts[j])
    norm = square
    for j in range(count):
        inner = -2.0 * products[j]
        for l in range(count):
            inner = inner + taken[l] * gram[j, l]
        norm = norm + taken[j] * inner
    return heights, taken, jnp.sqrt(jnp.maximum(norm, 0.0) + EPSILON)


def orthogonalized(vector, units, length):
    weights = []
    for e, unit in enumerate(units):
        used = min(e + 2, length)
        weight = sum(unit[j] * vector[j] for j in range(used))
        weights.append(weight)
        vector = [vector[j] - weight * unit[j] if j < used else vector[j] for j in range(length)]
    square = sum(entry * entry for entry in vector)
    size = jnp.sqrt(square)
    weights.append(size)
    return weights, [entry / size for entry in vector]


def solve_kernel(rows_ref, state_ref, f_ref, v_ref, z_ref, solution_ref, residual_ref):
    state = state_ref[...]
    known = ITERS - 2
    units = [[pick(state, UNIT[k, j]) for j in range(k + 2)] for k in range(known)]
    triangle = {(e, k): pick(state, UPPER[e, k]) for k in range(known) for e in range(k + 1)}
    beta = pick(state, BETA)
    dots = jnp.sum(rows_ref[...], axis=0, keepdims=True)
    gram, products, square = read_dots(dots, state, ITERS)
    heights, _, length = heights_of(gram, products, square, shifts_of(ITERS), ITERS)
    for k in range(known, ITERS):
        if k == ITERS - 1:
            vector = heights + [length]
        else:
            vector = [pick(state, HESS[j, k]) for j in range(k + 2)]
        weights, unit = orthogonalized(vector, units, k + 2)
        units.append(unit)
        triangle.update({(e, k): weights[e] for e in range(k + 1)})
    answers = [None] * ITERS
    for k in reversed(range(ITERS)):
        running = beta * units[k][0]
        for later in reversed(range(k + 1, ITERS)):
            running = running - triangle[k, later] * answers[later]
        answers[k] = running / triangle[k, k]
    result = answers[0] * v_ref[0]
    rest = f_ref[...] - answers[0] * z_ref[0]
    for k in range(1, ITERS):
        result = result + answers[k] * v_ref[k]
        rest = rest - answers[k] * z_ref[k]
    solution_ref[...] = result
    residual_ref[...] = rest


def on_device(
    forcing,
    stiffness,
    positions,
    far_weights,
    far_profile,
    near_blocks,
    near_dest,
    near_cilia,
    near_count,
):
    rows = lax.axis_size("row")
    cols = lax.axis_size("col")
    comps, cil, points = forcing.shape
    slots = near_blocks.shape[0]
    width = comps * points
    flat = comps * cil
    total = cil * rows * cols
    struct = lambda *shape, dtype=F32: jax.ShapeDtypeStruct(shape, dtype)
    vmem, smem, hbm = (pl.BlockSpec(memory_space=m) for m in (pltpu.VMEM, pltpu.SMEM, pltpu.HBM))
    slim = pltpu.CompilerParams(vmem_limit_bytes=4 << 20)
    roomy = pltpu.CompilerParams(vmem_limit_bytes=8 << 20)
    f = forcing.reshape(flat, points)
    stiff = stiffness.reshape(1, cil)
    weights = far_weights.reshape(1, points)
    profile = far_profile.reshape(1, points)
    in_hbm = lambda array: pltpu.with_memory_space_constraint(array, pltpu.HBM)
    blocks = in_hbm(near_blocks)
    cilia = in_hbm(near_cilia.T)
    dest = in_hbm(near_dest.reshape(slots))


    def exchange(send, x, kept, first):
        arrived = lax.all_to_all(send, "row", split_axis=0, concat_axis=0, tiled=True)
        outs, specs = [struct(cols, TILE, LANES, dtype=BF16)], [vmem]
        if first:
            table, extra = dest, ()
            outs += [pltpu.VMEM((KEPT, width, width), BF16), struct(slots, dtype=jnp.int32)]
            specs += [vmem, smem]
        else:
            table, extra = in_hbm(kept[1]), kept[:1]
        near, *fetched = pl.pallas_call(
            functools.partial(near_kernel, comps, cil, first),
            out_shape=outs,
            in_specs=[hbm, hbm, smem, vmem, hbm] + [vmem] * len(extra),
            out_specs=specs,
            scratch_shapes=[
                pltpu.VMEM((cil, TILE, width), BF16),
                pltpu.VMEM((cols * TILE, points), F32),
                pltpu.SMEM((cols,), jnp.int32),
                pltpu.VMEM((slots - KEPT, width, width), BF16),
                pltpu.SMEM(cilia.shape, jnp.int32),
                pltpu.SMEM(dest.shape, jnp.int32),
                pltpu.SemaphoreType.DMA((2 * len(CHUNKS),)),
                pltpu.SemaphoreType.DMA((2,)),
            ],
            compiler_params=pltpu.CompilerParams(vmem_limit_bytes=16 << 20),
            name="near",
        )(cilia, table, near_count, x, blocks, *extra)
        out = pl.pallas_call(
            functools.partial(join_kernel, comps, first),
            out_shape=struct(cols, PITCH[first], LANES, dtype=BF16),
            compiler_params=slim,
            name="join",
        )(arrived, near)
        recv = lax.all_to_all(out, "col", split_axis=0, concat_axis=0, tiled=True)
        return recv.reshape(cols * PITCH[first], LANES), fetched if first else kept

    send, x = pl.pallas_call(
        functools.partial(first_kernel, comps, cil),
        out_shape=[struct(rows, TILE, LANES), struct(flat, points)],
        in_specs=[hbm, hbm, hbm],
        out_specs=[vmem, vmem],
        scratch_shapes=[
            pltpu.VMEM((comps, cil), F32),
            pltpu.VMEM((1, points), F32),
            pltpu.SemaphoreType.DMA((comps,)),
        ],
        compiler_params=slim,
        name="first",
    )(in_hbm(f), in_hbm(positions), in_hbm(weights))
    recv, kept = exchange(send, x, None, True)
    sorted_rows = flat + comps * cols + TILE
    for step in range(1, ITERS + 1):
        first, last = step == 1, step == ITERS
        ins = [recv, x, stiff, profile]
        if not last:
            ins.append(weights)
        ins += [positions] if first else [sort, pairs, state, vs, zs]
        outs = []
        if first:
            outs += [
                struct(sorted_rows, cols * PITCH[False], dtype=BF16),
                struct(1 + comps, cols, cil, LANES),
            ]
        outs += [
            struct(rows * cols, LANES) if last else struct(rows, TILE, LANES),
            struct(flat, points),
            struct(step, flat, points),
            struct(step, flat, points),
            struct(1, LANES),
        ]
        results = pl.pallas_call(
            functools.partial(krylov_kernel, comps, cil, cols, total, step),
            out_shape=outs,
            scratch_shapes=[pltpu.VMEM((sorted_rows + comps * cols * first, LANES), F32)],
            compiler_params=roomy,
            name="krylov",
        )(*ins)
        if first:
            sort, pairs = results[:2]
            results = results[2:]
        send, x, vs, zs, state = results
        if not last:
            recv, _ = exchange(send, x, kept, False)
    everyone = lax.all_to_all(send, ("row", "col"), split_axis=0, concat_axis=0, tiled=True)
    out, rest = pl.pallas_call(
        solve_kernel, out_shape=[struct(flat, points)] * 2, compiler_params=slim, name="solve"
    )(everyone, state, f, vs, zs)
    return out.reshape(forcing.shape), rest.reshape(forcing.shape)


def solution(mesh):
    in_specs = (
        P(None, ("row", "col"), None),
        P(("row", "col")),
        P(None, ("row", "col")),
        P(),
        P(),
        P(("row", "col"), None, None),
        P(("row", "col"), None),
        P(("row", "col"), None),
        P(("row", "col")),
    )
    out_specs = (P(None, ("row", "col"), None), P(None, ("row", "col"), None))
    return jax.shard_map(
        on_device, mesh=mesh, in_specs=in_specs, out_specs=out_specs, check_vma=False
    )
```

```python
import functools
import jax
import jax.numpy as jnp
from jax import lax
from jax.experimental import pallas as pl
from jax.experimental.pallas import tpu as pltpu
from jax.sharding import PartitionSpec as P

CAPD = 2
ITERS = 4
EPSILON = 1e-06
F32 = jnp.float32
BF16 = jnp.bfloat16
HIGHEST = lax.Precision.HIGHEST
LANES = 128
GRAM = {(j, l): l * (l + 1) // 2 + j for l in range(ITERS) for j in range(l + 1)}
HESS = {(j, k): 16 + 8 * k + j for k in range(ITERS) for j in range(k + 2)}
BETA = 63
UPPER = {(e, k): 64 + 4 * k + e for k in range(ITERS) for e in range(k + 1)}
UNIT = {(k, j): 80 + 8 * k + j for k in range(ITERS) for j in range(k + 2)}
SHIFT = 2.0


def lane_iota(shape):
    return lax.broadcasted_iota(jnp.int32, shape, len(shape) - 1)


def column(row, size):
    eye = lax.broadcasted_iota(jnp.int32, (size, size), 0) == lane_iota((size, size))
    return jnp.sum(jnp.where(eye, row, 0.0), axis=1, keepdims=True)


def tall(col, comps):
    return jnp.concatenate([col] * comps, axis=0)


def bend(x, stiff):
    points = x.shape[1]
    lane = lane_iota(x.shape)

    def shifted(by):
        moved = pltpu.roll(x, by % points, 1)
        keep = lane >= by if by > 0 else lane < points + by
        return jnp.where(keep, moved, 0.0)

    fourth = shifted(2) - 4.0 * shifted(1) + 6.0 * x - 4.0 * shifted(-1) + shifted(-2)
    return x + stiff * fourth


def placed(x, weights, place, comps, cil):
    sums = jnp.sum(x * weights, axis=1, keepdims=True)
    return [
        jnp.sum(sums[i * cil:(i + 1) * cil] * place, axis=0, keepdims=True) for i in range(comps)
    ]


def place_of(cil):
    shape = (cil, LANES)
    own = lax.axis_index("row") * cil + lax.broadcasted_iota(jnp.int32, shape, 0)
    return jnp.where(lane_iota(shape) == own, 1.0, 0.0)


def to_every(send_ref, parts):
    if len(send_ref.shape) == 2:
        send_ref[...] = jnp.broadcast_to(parts[0], send_ref.shape)
        return
    rows = list(parts)
    rows += [jnp.zeros((1, LANES), F32)] * (send_ref.shape[1] - len(rows))
    tile = jnp.concatenate(rows, axis=0)
    send_ref[...] = jnp.broadcast_to(tile[None], send_ref.shape)


def dot_row(pairs):
    rows = [jnp.sum(a * b, axis=0, keepdims=True) for a, b in pairs]
    while len(rows) % 8:
        rows.append(jnp.zeros_like(rows[0]))
    sums = jnp.sum(jnp.concatenate(rows, axis=0), axis=1, keepdims=True)
    shape = (len(rows), LANES)
    eye = lax.broadcasted_iota(jnp.int32, shape, 0) == lane_iota(shape)
    return jnp.sum(jnp.where(eye, sums, 0.0), axis=0, keepdims=True)


def pick(row, lane):
    return jnp.broadcast_to(row[:, lane:lane + 1], row.shape)


def pack(entries):
    lane = lane_iota((1, LANES))
    row = jnp.zeros((1, LANES), F32)
    for where, value in entries.items():
        row = jnp.where(lane == where, value, row)
    return row


def first_kernel(comps, cil, f_hbm, pos_hbm, w_hbm, send_ref, x_out, pos_ref, w_ref, sems):
    copies = [
        pltpu.make_async_copy(source, target, sems.at[n])
        for n, (source, target) in enumerate(((f_hbm, x_out), (pos_hbm, pos_ref), (w_hbm, w_ref)))
    ]
    for copy in copies:
        copy.start()
    place = place_of(cil)
    for copy in copies:
        copy.wait()
    f = x_out[...]
    parts = placed(f, w_ref[...], place, comps, cil)
    parts.append(dot_row([(f, f)]))
    for i in range(comps):
        col = column(pos_ref[i:i + 1, :], cil)
        parts.append(jnp.sum(col * place, axis=0, keepdims=True))
    to_every(send_ref, parts)


TILE = 8
KEPT = 6
CHUNKS = (8, 8, 8, 8)
META = 6
DOTS = 14
PITCH = {True: 24, False: 16}


def near_kernel(comps, cil, first, cilia_hbm, table_hbm, count_ref, x_ref, b_ref, *refs):
    refs = list(refs)
    if not first:
        kept = refs.pop(0)
    out_ref = refs.pop(0)
    if first:
        kept, place_ref = refs[:2]
        refs = refs[2:]
    lhs, result, used, held, cilia_ref, table_ref, sems, table_sems = refs
    points = x_ref.shape[1]
    slots = b_ref.shape[0]
    bounds = [(sum(CHUNKS[:n]), sum(CHUNKS[:n + 1])) for n in range(len(CHUNKS))]

    def block(slot):
        return kept[slot] if slot < KEPT else held[slot - KEPT]

    def fetches(n):
        start, stop = bounds[n]
        parts = []
        if first and start < KEPT:
            parts.append((start, min(stop, KEPT), kept, 0))
        if stop > KEPT:
            parts.append((max(start, KEPT), stop, held, KEPT))
        return [
            pltpu.make_async_copy(
                b_ref.at[pl.ds(begin, end - begin)],
                target.at[pl.ds(begin - offset, end - begin)],
                sems.at[n + (target is kept) * len(CHUNKS)],
            )
            for begin, end, target, offset in parts
        ]

    tables = [
        pltpu.make_async_copy(source, target, table_sems.at[n])
        for n, (source, target) in enumerate(((cilia_hbm, cilia_ref), (table_hbm, table_ref)))
    ]
    for copy in tables:
        copy.start()
    for n in range(len(CHUNKS)):
        for copy in fetches(n):
            copy.start()
    result[...] = jnp.zeros_like(result)
    x = x_ref[...]
    high = x.astype(BF16).astype(F32)
    low = x - high
    row = lax.broadcasted_iota(jnp.int32, (TILE, points), 0)
    for g in range(cil):
        for i in range(comps):
            at = i * cil + g
            value = jnp.where(row == 0, high[at:at + 1], jnp.where(row == 1, low[at:at + 1], 0.0))
            lhs[g, :, i * points:(i + 1) * points] = value.astype(BF16)
    for copy in tables:
        copy.wait()
    if first:
        lane = lane_iota((1, points))
        for dest in range(used.shape[0]):
            used[dest] = 0
        for slot in range(slots):
            dest = table_ref[slot]
            rank = used[dest]
            used[dest] = rank + 1
            place_ref[slot] = dest * TILE + rank * comps
            at = pl.ds(dest * TILE + META, 1)
            target = cilia_ref[1, slot].astype(F32)
            result[at, :] = jnp.where(lane == rank, target, result[at, :])
    else:
        place_ref = table_ref
    for n, (start, stop) in enumerate(bounds):
        for copy in fetches(n):
            copy.wait()
        speeds = [
            lax.dot_general(
                lhs[cilia_ref[0, slot]], block(slot), (((1,), (1,)), ((), ())),
                preferred_element_type=F32,
            )
            for slot in range(start, stop)
        ]
        for slot, speed in zip(range(start, stop), speeds):
            speed = jnp.where(slot < count_ref[0], speed[0:1] + speed[1:2], 0.0)
            for i in range(comps):
                result[pl.ds(place_ref[slot] + i, 1), :] = speed[:, i * points:(i + 1) * points]
    out_ref[...] = result[...].astype(BF16).reshape(out_ref.shape)


def join_kernel(comps, first, rows_ref, near_ref, send_ref):
    total = jnp.sum(rows_ref[...], axis=0)
    high = total.astype(BF16).astype(F32)
    rest = total - high
    middle = rest.astype(BF16).astype(F32)
    low = rest - middle
    at = comps
    shared = jnp.concatenate(
        [
            high[:at], rest[:at], high[at:at + 1],
            middle[at:at + 1] + pltpu.roll(low[at:at + 1], LANES // 2, 1),
        ],
        axis=0,
    )
    send_ref[:, :TILE, :] = near_ref[...]
    send_ref[:, TILE:2 * TILE, :] = jnp.broadcast_to(
        shared.astype(BF16)[None], (send_ref.shape[0],) + shared.shape
    )
    if first:
        at = comps + 1
        places = jnp.concatenate(
            [high[at:at + comps], rest[at:at + comps], jnp.zeros((TILE - 2 * comps, LANES), F32)], axis=0
        )
        send_ref[:, 2 * TILE:3 * TILE, :] = jnp.broadcast_to(
            places.astype(BF16)[None], (send_ref.shape[0],) + places.shape
        )


def sorting(comps, cil, sources, pitch, targets):
    def parts(rows):
        shape = (rows, sources * pitch)
        row = lax.broadcasted_iota(jnp.int32, shape, 0)
        lane = lane_iota(shape)
        return row, lax.div(lane, pitch), lax.rem(lane, pitch)

    row, _, place = parts(comps * cil)
    comp, cilium = lax.div(row, cil), lax.rem(row, cil).astype(F32)
    found = jnp.zeros(row.shape, jnp.bool_)
    for rank in range(CAPD):
        found |= (place == rank * comps + comp) & (cilium == targets[rank])
    pieces = [found]

    def gathered(start):
        row, source, place = parts(comps * sources)
        comp, wanted = lax.div(row, sources), lax.rem(row, sources)
        here = (place == start + comp) | (place == start + comps + comp)
        return here & (source == wanted)

    pieces.append(gathered(TILE))
    row, _, place = parts(TILE)
    pieces.append((row == 0) & ((place == DOTS) | (place == DOTS + 1)))
    if pitch > 2 * TILE:
        pieces.append(gathered(2 * TILE))
    return jnp.concatenate([jnp.where(p, 1.0, 0.0) for p in pieces], axis=0).astype(BF16)


def applied(x, stiff, rows, pairs, profile, comps, cil, sources):
    flat = comps * cil
    image = bend(x, stiff) + rows[:flat]
    totals = [jnp.zeros((cil, LANES), F32) for _ in range(comps)]
    for s in range(sources):
        strength = [rows[flat + j * sources + s:flat + j * sources + s + 1] for j in range(comps)]
        along = [pairs(1 + j, s) for j in range(comps)]
        projected = sum(along[j] * strength[j] for j in range(comps))
        direct = pairs(0, s)
        for i in range(comps):
            totals[i] = totals[i] + (direct * strength[i] + along[i] * projected)
    far = jnp.concatenate([jnp.sum(t, axis=1, keepdims=True) for t in totals], axis=0)
    dots = rows[flat + comps * sources:flat + comps * sources + 1]
    dots = dots + pltpu.roll(dots, LANES // 2, 1)
    return image + far * profile, dots


def krylov_kernel(comps, cil, sources, total, step, *refs):
    first = step == 1
    last = step == ITERS
    refs = list(refs)
    recv_ref, x_ref, stiff_ref, prof_ref = refs[:4]
    refs = refs[4:]
    if not last:
        w_ref = refs.pop(0)
    if first:
        pos_ref = refs.pop(0)
    else:
        sort_ref, pairs_ref, state_ref, v_ref, z_ref = refs[:5]
        refs = refs[5:]
    if first:
        sort_out, pairs_out = refs[:2]
        refs = refs[2:]
    send_ref, x_out, v_out, z_out, state_out, rows = refs
    x = x_ref[...]
    flat = comps * cil
    stiff = tall(column(stiff_ref[...], cil), comps)

    if first:
        pitch = PITCH[True]
        arrived = recv_ref[...]
        shape = (sources, sources * pitch)
        source, lane = lax.broadcasted_iota(jnp.int32, shape, 0), lane_iota(shape)
        chosen = jnp.where(lane == source * pitch + META, 1.0, 0.0).astype(BF16)
        meta = jnp.dot(chosen, arrived, preferred_element_type=F32)
        eye = lax.broadcasted_iota(jnp.int32, (sources, sources), 0) == lane_iota((sources, sources))
        named = [
            jnp.sum(jnp.where(eye, meta[:, rank:rank + 1], 0.0), axis=0, keepdims=True) for rank in range(CAPD)
        ]
        named = jnp.concatenate(
            [jnp.broadcast_to(n, (TILE, sources)) for n in named], axis=0
        ).astype(BF16)

        def targets_for(pitch):
            shape = (sources, sources * pitch)
            source, lane = lax.broadcasted_iota(jnp.int32, shape, 0), lane_iota(shape)
            spread = jnp.where(lax.div(lane, pitch) == source, 1.0, 0.0).astype(BF16)
            wide = jnp.dot(named, spread, preferred_element_type=F32)
            return [wide[rank * TILE:rank * TILE + 1] for rank in range(CAPD)]

        sort_out[...] = sorting(comps, cil, sources, PITCH[False], targets_for(PITCH[False]))
        sort = sorting(comps, cil, sources, pitch, targets_for(pitch))
        rows[...] = jnp.dot(sort, arrived, preferred_element_type=F32)
        eps_three = 4.0 / total
        eps_two = eps_three ** (2.0 / 3.0)
        here = [
            jnp.broadcast_to(column(pos_ref[i:i + 1, :], cil), (cil, LANES)) for i in range(comps)
        ]
        start = flat + comps * sources + TILE
        for s in range(sources):
            gap = [
                here[i] - rows[start + i * sources + s:start + i * sources + s + 1]
                for i in range(comps)
            ]
            inverse = 1.0 / (gap[0] * gap[0] + gap[1] * gap[1] + gap[2] * gap[2] + eps_two)
            amplitude = eps_three * inverse * jnp.sqrt(inverse)
            slope = jnp.sqrt(amplitude * inverse)
            pairs_out[0, s] = amplitude
            for i in range(comps):
                pairs_out[1 + i, s] = slope * gap[i]
        pairs = lambda at, s: pairs_out[at, s]
    else:
        rows[...] = jnp.dot(sort_ref[...], recv_ref[...], preferred_element_type=F32)
        pairs = lambda at, s: pairs_ref[at, s]

    image, dots = applied(x, stiff, rows, pairs, prof_ref[...], comps, cil, sources)
    entries = {}
    if first:
        beta = jnp.sqrt(pick(dots, 0) + EPSILON)
        entries[BETA] = beta
        scale = 1.0 / beta
        basis = [x * scale]
        images = [image * scale]
    else:
        state = state_ref[...]
        count = step - 1
        gram, products, square = read_dots(dots, state, count)
        basis = [v_ref[j] for j in range(count)]
        images = [z_ref[j] for j in range(count)]
        heights, taken, length = heights_of(gram, products, square, shifts_of(count), count)
        scale = 1.0 / length
        vector, product = x, image
        for j in range(count):
            vector = vector - taken[j] * basis[j]
            product = product - taken[j] * images[j]
        basis.append(vector * scale)
        images.append(product * scale)
        for j in range(count):
            entries[GRAM[j, count - 1]] = gram[j, count - 1]
            entries[HESS[j, count - 1]] = heights[j]
        entries[HESS[count, count - 1]] = length
        if last:
            units = []
            for k in range(count - 1):
                vector = [pick(state, HESS[j, k]) for j in range(k + 2)]
                weights, unit = orthogonalized(vector, units, k + 2)
                units.append(unit)
                entries.update({UPPER[e, k]: weights[e] for e in range(k + 1)})
                entries.update({UNIT[k, j]: unit[j] for j in range(k + 2)})
    row = pack(entries)
    state_out[...] = row if first else row + state
    for j in range(step):
        v_out[j] = basis[j]
        z_out[j] = images[j]
    outgoing = images[-1]
    for j, shift in enumerate(shifts_of(step)):
        if shift:
            outgoing = outgoing - shift * basis[j]
    pairs_of_dots = [(basis[j], basis[-1]) for j in range(step)]
    pairs_of_dots += [(basis[j], outgoing) for j in range(step)]
    pairs_of_dots.append((outgoing, outgoing))
    local = dot_row(pairs_of_dots)
    if last:
        to_every(send_ref, [local])
    else:
        to_every(send_ref, placed(outgoing, w_ref[...], place_of(cil), comps, cil) + [local])
    x_out[...] = outgoing


def shifts_of(count):
    if count == ITERS:
        return [0.0] * count
    return [0.0] * (count - 1) + [SHIFT]


def read_dots(dots, state, count):
    gram = {}
    for l in range(count):
        for j in range(l + 1):
            gram[j, l] = pick(dots, j) if l == count - 1 else pick(state, GRAM[j, l])
            gram[l, j] = gram[j, l]
    return gram, [pick(dots, count + j) for j in range(count)], pick(dots, 2 * count)


def heights_of(gram, products, square, shifts, count):
    heights, taken = [], []
    for j in range(count):
        extra = sum((shifts[l] * gram[j, l] for l in range(count) if shifts[l]), 0.0)
        heights.append(products[j] + extra)
        taken.append(heights[j] - shifts[j])
    norm = square
    for j in range(count):
        inner = -2.0 * products[j]
        for l in range(count):
            inner = inner + taken[l] * gram[j, l]
        norm = norm + taken[j] * inner
    return heights, taken, jnp.sqrt(jnp.maximum(norm, 0.0) + EPSILON)


def orthogonalized(vector, units, length):
    weights = []
    for e, unit in enumerate(units):
        used = min(e + 2, length)
        weight = sum(unit[j] * vector[j] for j in range(used))
        weights.append(weight)
        vector = [vector[j] - weight * unit[j] if j < used else vector[j] for j in range(length)]
    square = sum(entry * entry for entry in vector)
    size = jnp.sqrt(square)
    weights.append(size)
    inverse = 1.0 / size
    return weights, [entry * inverse for entry in vector]


def solve_kernel(rows_ref, state_ref, f_ref, v_ref, z_ref, solution_ref, residual_ref):
    state = state_ref[...]
    known = ITERS - 2
    units = [[pick(state, UNIT[k, j]) for j in range(k + 2)] for k in range(known)]
    triangle = {(e, k): pick(state, UPPER[e, k]) for k in range(known) for e in range(k + 1)}
    beta = pick(state, BETA)
    dots = jnp.sum(rows_ref[...], axis=0, keepdims=True)
    gram, products, square = read_dots(dots, state, ITERS)
    heights, _, length = heights_of(gram, products, square, shifts_of(ITERS), ITERS)
    for k in range(known, ITERS):
        if k == ITERS - 1:
            vector = heights + [length]
        else:
            vector = [pick(state, HESS[j, k]) for j in range(k + 2)]
        weights, unit = orthogonalized(vector, units, k + 2)
        units.append(unit)
        triangle.update({(e, k): weights[e] for e in range(k + 1)})
    inverses = [1.0 / triangle[k, k] for k in range(ITERS)]
    answers = [None] * ITERS
    for k in reversed(range(ITERS)):
        running = beta * units[k][0]
        for later in reversed(range(k + 1, ITERS)):
            running = running - triangle[k, later] * answers[later]
        answers[k] = running * inverses[k]
    result = answers[0] * v_ref[0]
    rest = f_ref[...] - answers[0] * z_ref[0]
    for k in range(1, ITERS):
        result = result + answers[k] * v_ref[k]
        rest = rest - answers[k] * z_ref[k]
    solution_ref[...] = result
    residual_ref[...] = rest


def on_device(
    forcing,
    stiffness,
    positions,
    far_weights,
    far_profile,
    near_blocks,
    near_dest,
    near_cilia,
    near_count,
):
    rows = lax.axis_size("row")
    cols = lax.axis_size("col")
    comps, cil, points = forcing.shape
    slots = near_blocks.shape[0]
    width = comps * points
    flat = comps * cil
    total = cil * rows * cols
    struct = lambda *shape, dtype=F32: jax.ShapeDtypeStruct(shape, dtype)
    vmem, smem, hbm = (pl.BlockSpec(memory_space=m) for m in (pltpu.VMEM, pltpu.SMEM, pltpu.HBM))
    slim = pltpu.CompilerParams(vmem_limit_bytes=4 << 20)
    roomy = pltpu.CompilerParams(vmem_limit_bytes=8 << 20)
    f = forcing.reshape(flat, points)
    stiff = stiffness.reshape(1, cil)
    weights = far_weights.reshape(1, points)
    profile = far_profile.reshape(1, points)
    in_hbm = lambda array: pltpu.with_memory_space_constraint(array, pltpu.HBM)
    blocks = in_hbm(near_blocks)
    cilia = in_hbm(near_cilia.T)
    dest = in_hbm(near_dest.reshape(slots))


    def exchange(send, x, kept, first):
        arrived = lax.all_to_all(send, "row", split_axis=0, concat_axis=0, tiled=True)
        outs, specs = [struct(cols, TILE, LANES, dtype=BF16)], [vmem]
        if first:
            table, extra = dest, ()
            outs += [pltpu.VMEM((KEPT, width, width), BF16), struct(slots, dtype=jnp.int32)]
            specs += [vmem, smem]
        else:
            table, extra = in_hbm(kept[1]), kept[:1]
        near, *fetched = pl.pallas_call(
            functools.partial(near_kernel, comps, cil, first),
            out_shape=outs,
            in_specs=[hbm, hbm, smem, vmem, hbm] + [vmem] * len(extra),
            out_specs=specs,
            scratch_shapes=[
                pltpu.VMEM((cil, TILE, width), BF16),
                pltpu.VMEM((cols * TILE, points), F32),
                pltpu.SMEM((cols,), jnp.int32),
                pltpu.VMEM((slots - KEPT, width, width), BF16),
                pltpu.SMEM(cilia.shape, jnp.int32),
                pltpu.SMEM(dest.shape, jnp.int32),
                pltpu.SemaphoreType.DMA((2 * len(CHUNKS),)),
                pltpu.SemaphoreType.DMA((2,)),
            ],
            compiler_params=pltpu.CompilerParams(vmem_limit_bytes=16 << 20),
            name="near",
        )(cilia, table, near_count, x, blocks, *extra)
        out = pl.pallas_call(
            functools.partial(join_kernel, comps, first),
            out_shape=struct(cols, PITCH[first], LANES, dtype=BF16),
            compiler_params=slim,
            name="join",
        )(arrived, near)
        recv = lax.all_to_all(out, "col", split_axis=0, concat_axis=0, tiled=True)
        return recv.reshape(cols * PITCH[first], LANES), fetched if first else kept

    send, x = pl.pallas_call(
        functools.partial(first_kernel, comps, cil),
        out_shape=[struct(rows, TILE, LANES), struct(flat, points)],
        in_specs=[hbm, hbm, hbm],
        out_specs=[vmem, vmem],
        scratch_shapes=[
            pltpu.VMEM((comps, cil), F32),
            pltpu.VMEM((1, points), F32),
            pltpu.SemaphoreType.DMA((comps,)),
        ],
        compiler_params=slim,
        name="first",
    )(in_hbm(f), in_hbm(positions), in_hbm(weights))
    recv, kept = exchange(send, x, None, True)
    sorted_rows = flat + comps * cols + TILE
    for step in range(1, ITERS + 1):
        first, last = step == 1, step == ITERS
        ins = [recv, x, stiff, profile]
        if not last:
            ins.append(weights)
        ins += [positions] if first else [sort, pairs, state, vs, zs]
        outs = []
        if first:
            outs += [
                struct(sorted_rows, cols * PITCH[False], dtype=BF16),
                struct(1 + comps, cols, cil, LANES),
            ]
        outs += [
            struct(rows * cols, LANES) if last else struct(rows, TILE, LANES),
            struct(flat, points),
            struct(step, flat, points),
            struct(step, flat, points),
            struct(1, LANES),
        ]
        results = pl.pallas_call(
            functools.partial(krylov_kernel, comps, cil, cols, total, step),
            out_shape=outs,
            scratch_shapes=[pltpu.VMEM((sorted_rows + comps * cols * first, LANES), F32)],
            compiler_params=roomy,
            name="krylov",
        )(*ins)
        if first:
            sort, pairs = results[:2]
            results = results[2:]
        send, x, vs, zs, state = results
        if not last:
            recv, _ = exchange(send, x, kept, False)
    everyone = lax.all_to_all(send, ("row", "col"), split_axis=0, concat_axis=0, tiled=True)
    out, rest = pl.pallas_call(
        solve_kernel, out_shape=[struct(flat, points)] * 2, compiler_params=slim, name="solve"
    )(everyone, state, f, vs, zs)
    return out.reshape(forcing.shape), rest.reshape(forcing.shape)


def solution(mesh):
    in_specs = (
        P(None, ("row", "col"), None),
        P(("row", "col")),
        P(None, ("row", "col")),
        P(),
        P(),
        P(("row", "col"), None, None),
        P(("row", "col"), None),
        P(("row", "col"), None),
        P(("row", "col")),
    )
    out_specs = (P(None, ("row", "col"), None), P(None, ("row", "col"), None))
    return jax.shard_map(
        on_device, mesh=mesh, in_specs=in_specs, out_specs=out_specs, check_vma=False
    )
```

```python
import functools
import jax
import jax.numpy as jnp
from jax import lax
from jax.experimental import pallas as pl
from jax.experimental.pallas import tpu as pltpu
from jax.sharding import PartitionSpec as P

CAPD = 2
ITERS = 4
EPSILON = 1e-06
F32 = jnp.float32
BF16 = jnp.bfloat16
HIGHEST = lax.Precision.HIGHEST
LANES = 128
GRAM = {(j, l): l * (l + 1) // 2 + j for l in range(ITERS) for j in range(l + 1)}
HESS = {(j, k): 16 + 8 * k + j for k in range(ITERS) for j in range(k + 2)}
BETA = 63
UPPER = {(e, k): 64 + 4 * k + e for k in range(ITERS) for e in range(k + 1)}
UNIT = {(k, j): 80 + 8 * k + j for k in range(ITERS) for j in range(k + 2)}
SHIFT = 2.0


def lane_iota(shape):
    return lax.broadcasted_iota(jnp.int32, shape, len(shape) - 1)


def column(row, size):
    eye = lax.broadcasted_iota(jnp.int32, (size, size), 0) == lane_iota((size, size))
    return jnp.sum(jnp.where(eye, row, 0.0), axis=1, keepdims=True)


def tall(col, comps):
    return jnp.concatenate([col] * comps, axis=0)


def bend(x, stiff):
    points = x.shape[1]
    lane = lane_iota(x.shape)

    def shifted(by):
        moved = pltpu.roll(x, by % points, 1)
        keep = lane >= by if by > 0 else lane < points + by
        return jnp.where(keep, moved, 0.0)

    fourth = shifted(2) - 4.0 * shifted(1) + 6.0 * x - 4.0 * shifted(-1) + shifted(-2)
    return x + stiff * fourth


def placed(x, weights, place, comps, cil):
    sums = jnp.sum(x * weights, axis=1, keepdims=True)
    return [
        jnp.sum(sums[i * cil:(i + 1) * cil] * place, axis=0, keepdims=True) for i in range(comps)
    ]


def place_of(cil):
    shape = (cil, LANES)
    own = lax.axis_index("row") * cil + lax.broadcasted_iota(jnp.int32, shape, 0)
    return jnp.where(lane_iota(shape) == own, 1.0, 0.0)


def to_every(send_ref, parts):
    if len(send_ref.shape) == 2:
        send_ref[...] = jnp.broadcast_to(parts[0], send_ref.shape)
        return
    rows = list(parts)
    rows += [jnp.zeros((1, LANES), F32)] * (send_ref.shape[1] - len(rows))
    tile = jnp.concatenate(rows, axis=0)
    send_ref[...] = jnp.broadcast_to(tile[None], send_ref.shape)


def dot_row(pairs):
    rows = [jnp.sum(a * b, axis=0, keepdims=True) for a, b in pairs]
    while len(rows) % 8:
        rows.append(jnp.zeros_like(rows[0]))
    sums = jnp.sum(jnp.concatenate(rows, axis=0), axis=1, keepdims=True)
    shape = (len(rows), LANES)
    eye = lax.broadcasted_iota(jnp.int32, shape, 0) == lane_iota(shape)
    return jnp.sum(jnp.where(eye, sums, 0.0), axis=0, keepdims=True)


def pick(row, lane):
    return jnp.broadcast_to(row[:, lane:lane + 1], row.shape)


def pack(entries):
    lane = lane_iota((1, LANES))
    row = jnp.zeros((1, LANES), F32)
    for where, value in entries.items():
        row = jnp.where(lane == where, value, row)
    return row


def first_kernel(comps, cil, f_hbm, pos_hbm, w_hbm, send_ref, x_out, pos_ref, w_ref, sems):
    copies = [
        pltpu.make_async_copy(source, target, sems.at[n])
        for n, (source, target) in enumerate(((f_hbm, x_out), (pos_hbm, pos_ref), (w_hbm, w_ref)))
    ]
    for copy in copies:
        copy.start()
    place = place_of(cil)
    for copy in copies:
        copy.wait()
    f = x_out[...]
    parts = placed(f, w_ref[...], place, comps, cil)
    parts.append(dot_row([(f, f)]))
    for i in range(comps):
        col = column(pos_ref[i:i + 1, :], cil)
        parts.append(jnp.sum(col * place, axis=0, keepdims=True))
    to_every(send_ref, parts)


TILE = 8
KEPT = 6
CHUNKS = (8, 8, 8, 8)
META = 6
DOTS = 14
PITCH = {True: 24, False: 16}


def near_kernel(comps, cil, first, cilia_hbm, table_hbm, count_ref, x_ref, b_ref, *refs):
    refs = list(refs)
    if not first:
        kept = refs.pop(0)
    out_ref = refs.pop(0)
    if first:
        kept, place_ref = refs[:2]
        refs = refs[2:]
    lhs, result, used, held, cilia_ref, table_ref, sems, table_sems = refs
    points = x_ref.shape[1]
    slots = b_ref.shape[0]
    bounds = [(sum(CHUNKS[:n]), sum(CHUNKS[:n + 1])) for n in range(len(CHUNKS))]

    def block(slot):
        return kept[slot] if slot < KEPT else held[slot - KEPT]

    def fetches(n):
        start, stop = bounds[n]
        parts = []
        if first and start < KEPT:
            parts.append((start, min(stop, KEPT), kept, 0))
        if stop > KEPT:
            parts.append((max(start, KEPT), stop, held, KEPT))
        return [
            pltpu.make_async_copy(
                b_ref.at[pl.ds(begin, end - begin)],
                target.at[pl.ds(begin - offset, end - begin)],
                sems.at[n + (target is kept) * len(CHUNKS)],
            )
            for begin, end, target, offset in parts
        ]

    tables = [
        pltpu.make_async_copy(source, target, table_sems.at[n])
        for n, (source, target) in enumerate(((cilia_hbm, cilia_ref), (table_hbm, table_ref)))
    ]
    for copy in tables:
        copy.start()
    for n in range(len(CHUNKS)):
        for copy in fetches(n):
            copy.start()
    result[...] = jnp.zeros_like(result)
    x = x_ref[...]
    high = x.astype(BF16).astype(F32)
    low = x - high
    row = lax.broadcasted_iota(jnp.int32, (TILE, points), 0)
    for g in range(cil):
        for i in range(comps):
            at = i * cil + g
            value = jnp.where(row == 0, high[at:at + 1], jnp.where(row == 1, low[at:at + 1], 0.0))
            lhs[g, :, i * points:(i + 1) * points] = value.astype(BF16)
    for copy in tables:
        copy.wait()
    if first:
        lane = lane_iota((1, points))
        for dest in range(used.shape[0]):
            used[dest] = 0
        for slot in range(slots):
            dest = table_ref[slot]
            rank = used[dest]
            used[dest] = rank + 1
            place_ref[slot] = dest * TILE + rank * comps
            at = pl.ds(dest * TILE + META, 1)
            target = cilia_ref[1, slot].astype(F32)
            result[at, :] = jnp.where(lane == rank, target, result[at, :])
    else:
        place_ref = table_ref
    for n, (start, stop) in enumerate(bounds):
        for copy in fetches(n):
            copy.wait()
        speeds = [
            lax.dot_general(
                lhs[cilia_ref[0, slot]], block(slot), (((1,), (1,)), ((), ())),
                preferred_element_type=F32,
            )
            for slot in range(start, stop)
        ]
        for slot, speed in zip(range(start, stop), speeds):
            speed = jnp.where(slot < count_ref[0], speed[0:1] + speed[1:2], 0.0)
            for i in range(comps):
                result[pl.ds(place_ref[slot] + i, 1), :] = speed[:, i * points:(i + 1) * points]
    out_ref[...] = result[...].astype(BF16).reshape(out_ref.shape)


def join_kernel(comps, first, rows_ref, near_ref, send_ref):
    total = jnp.sum(rows_ref[...], axis=0)
    high = total.astype(BF16).astype(F32)
    rest = total - high
    middle = rest.astype(BF16).astype(F32)
    low = rest - middle
    at = comps
    shared = jnp.concatenate(
        [
            high[:at], rest[:at], high[at:at + 1],
            middle[at:at + 1] + pltpu.roll(low[at:at + 1], LANES // 2, 1),
        ],
        axis=0,
    )
    send_ref[:, :TILE, :] = near_ref[...]
    send_ref[:, TILE:2 * TILE, :] = jnp.broadcast_to(
        shared.astype(BF16)[None], (send_ref.shape[0],) + shared.shape
    )
    if first:
        at = comps + 1
        places = jnp.concatenate(
            [high[at:at + comps], rest[at:at + comps], jnp.zeros((TILE - 2 * comps, LANES), F32)], axis=0
        )
        send_ref[:, 2 * TILE:3 * TILE, :] = jnp.broadcast_to(
            places.astype(BF16)[None], (send_ref.shape[0],) + places.shape
        )


def sorting(comps, cil, sources, pitch, targets):
    def parts(rows):
        shape = (rows, sources * pitch)
        row = lax.broadcasted_iota(jnp.int32, shape, 0)
        lane = lane_iota(shape)
        return row, lax.div(lane, pitch), lax.rem(lane, pitch)

    row, _, place = parts(comps * cil)
    comp, cilium = lax.div(row, cil), lax.rem(row, cil).astype(F32)
    found = jnp.zeros(row.shape, jnp.bool_)
    for rank in range(CAPD):
        found |= (place == rank * comps + comp) & (cilium == targets[rank])
    pieces = [found]

    def gathered(start):
        row, source, place = parts(comps * sources)
        comp, wanted = lax.div(row, sources), lax.rem(row, sources)
        here = (place == start + comp) | (place == start + comps + comp)
        return here & (source == wanted)

    pieces.append(gathered(TILE))
    row, _, place = parts(TILE)
    pieces.append((row == 0) & ((place == DOTS) | (place == DOTS + 1)))
    if pitch > 2 * TILE:
        pieces.append(gathered(2 * TILE))
    return jnp.concatenate([jnp.where(p, 1.0, 0.0) for p in pieces], axis=0).astype(BF16)


def applied(x, stiff, rows, pairs, profile, comps, cil, sources):
    flat = comps * cil
    image = bend(x, stiff) + rows[:flat]
    totals = [jnp.zeros((cil, LANES), F32) for _ in range(comps)]
    for s in range(sources):
        strength = [rows[flat + j * sources + s:flat + j * sources + s + 1] for j in range(comps)]
        along = [pairs(1 + j, s) for j in range(comps)]
        projected = sum(along[j] * strength[j] for j in range(comps))
        direct = pairs(0, s)
        for i in range(comps):
            totals[i] = totals[i] + (direct * strength[i] + along[i] * projected)
    far = jnp.concatenate([jnp.sum(t, axis=1, keepdims=True) for t in totals], axis=0)
    dots = rows[flat + comps * sources:flat + comps * sources + 1]
    dots = dots + pltpu.roll(dots, LANES // 2, 1)
    return image + far * profile, dots


def krylov_kernel(comps, cil, sources, total, step, *refs):
    first = step == 1
    last = step == ITERS
    refs = list(refs)
    recv_ref, x_ref, stiff_ref, prof_ref = refs[:4]
    refs = refs[4:]
    if not last:
        w_ref = refs.pop(0)
    if first:
        pos_ref = refs.pop(0)
    else:
        sort_ref, pairs_ref, state_ref, v_ref, z_ref = refs[:5]
        refs = refs[5:]
    if first:
        sort_out, pairs_out = refs[:2]
        refs = refs[2:]
    send_ref, x_out, v_out, z_out, state_out, rows = refs
    x = x_ref[...]
    flat = comps * cil
    stiff = tall(column(stiff_ref[...], cil), comps)

    if first:
        pitch = PITCH[True]
        arrived = recv_ref[...]
        shape = (sources, sources * pitch)
        source, lane = lax.broadcasted_iota(jnp.int32, shape, 0), lane_iota(shape)
        chosen = jnp.where(lane == source * pitch + META, 1.0, 0.0).astype(BF16)
        meta = jnp.dot(chosen, arrived, preferred_element_type=F32)
        eye = lax.broadcasted_iota(jnp.int32, (sources, sources), 0) == lane_iota((sources, sources))
        named = [
            jnp.sum(jnp.where(eye, meta[:, rank:rank + 1], 0.0), axis=0, keepdims=True) for rank in range(CAPD)
        ]
        named = jnp.concatenate(
            [jnp.broadcast_to(n, (TILE, sources)) for n in named], axis=0
        ).astype(BF16)

        def targets_for(pitch):
            shape = (sources, sources * pitch)
            source, lane = lax.broadcasted_iota(jnp.int32, shape, 0), lane_iota(shape)
            spread = jnp.where(lax.div(lane, pitch) == source, 1.0, 0.0).astype(BF16)
            wide = jnp.dot(named, spread, preferred_element_type=F32)
            return [wide[rank * TILE:rank * TILE + 1] for rank in range(CAPD)]

        sort_out[...] = sorting(comps, cil, sources, PITCH[False], targets_for(PITCH[False]))
        sort = sorting(comps, cil, sources, pitch, targets_for(pitch))
        rows[...] = jnp.dot(sort, arrived, preferred_element_type=F32)
        eps_three = 4.0 / total
        eps_two = eps_three ** (2.0 / 3.0)
        here = [
            jnp.broadcast_to(column(pos_ref[i:i + 1, :], cil), (cil, LANES)) for i in range(comps)
        ]
        start = flat + comps * sources + TILE
        for s in range(sources):
            gap = [
                here[i] - rows[start + i * sources + s:start + i * sources + s + 1]
                for i in range(comps)
            ]
            inverse = 1.0 / (gap[0] * gap[0] + gap[1] * gap[1] + gap[2] * gap[2] + eps_two)
            amplitude = eps_three * inverse * jnp.sqrt(inverse)
            slope = jnp.sqrt(amplitude * inverse)
            pairs_out[0, s] = amplitude
            for i in range(comps):
                pairs_out[1 + i, s] = slope * gap[i]
        pairs = lambda at, s: pairs_out[at, s]
    else:
        rows[...] = jnp.dot(sort_ref[...], recv_ref[...], preferred_element_type=F32)
        pairs = lambda at, s: pairs_ref[at, s]

    image, dots = applied(x, stiff, rows, pairs, prof_ref[...], comps, cil, sources)
    entries = {}
    if first:
        beta = jnp.sqrt(pick(dots, 0) + EPSILON)
        entries[BETA] = beta
        scale = 1.0 / beta
        basis = [x * scale]
        images = [image * scale]
    else:
        state = state_ref[...]
        count = step - 1
        gram, products, square = read_dots(dots, state, count)
        basis = [v_ref[j] for j in range(count)]
        images = [z_ref[j] for j in range(count)]
        heights, taken, length = heights_of(gram, products, square, shifts_of(count), count)
        scale = 1.0 / length
        vector, product = x, image
        for j in range(count):
            vector = vector - taken[j] * basis[j]
            product = product - taken[j] * images[j]
        basis.append(vector * scale)
        images.append(product * scale)
        for j in range(count):
            entries[GRAM[j, count - 1]] = gram[j, count - 1]
            entries[HESS[j, count - 1]] = heights[j]
        entries[HESS[count, count - 1]] = length
        if last:
            units = []
            for k in range(count - 1):
                vector = [pick(state, HESS[j, k]) for j in range(k + 2)]
                weights, unit = orthogonalized(vector, units, k + 2)
                units.append(unit)
                entries.update({UPPER[e, k]: weights[e] for e in range(k + 1)})
                entries.update({UNIT[k, j]: unit[j] for j in range(k + 2)})
    row = pack(entries)
    state_out[...] = row if first else row + state
    for j in range(step):
        v_out[j] = basis[j]
        z_out[j] = images[j]
    outgoing = images[-1]
    for j, shift in enumerate(shifts_of(step)):
        if shift:
            outgoing = outgoing - shift * basis[j]
    pairs_of_dots = [(basis[j], basis[-1]) for j in range(step)]
    pairs_of_dots += [(basis[j], outgoing) for j in range(step)]
    pairs_of_dots.append((outgoing, outgoing))
    local = dot_row(pairs_of_dots)
    if last:
        to_every(send_ref, [local])
    else:
        to_every(send_ref, placed(outgoing, w_ref[...], place_of(cil), comps, cil) + [local])
    x_out[...] = outgoing


def shifts_of(count):
    if count == ITERS:
        return [0.0] * count
    return [0.0] * (count - 1) + [SHIFT]


def read_dots(dots, state, count):
    gram = {}
    for l in range(count):
        for j in range(l + 1):
            gram[j, l] = pick(dots, j) if l == count - 1 else pick(state, GRAM[j, l])
            gram[l, j] = gram[j, l]
    return gram, [pick(dots, count + j) for j in range(count)], pick(dots, 2 * count)


def heights_of(gram, products, square, shifts, count):
    heights, taken = [], []
    for j in range(count):
        extra = sum((shifts[l] * gram[j, l] for l in range(count) if shifts[l]), 0.0)
        heights.append(products[j] + extra)
        taken.append(heights[j] - shifts[j])
    norm = square
    for j in range(count):
        inner = -2.0 * products[j]
        for l in range(count):
            inner = inner + taken[l] * gram[j, l]
        norm = norm + taken[j] * inner
    return heights, taken, jnp.sqrt(jnp.maximum(norm, 0.0) + EPSILON)


def orthogonalized(vector, units, length):
    weights = []
    for e, unit in enumerate(units):
        used = min(e + 2, length)
        weight = sum(unit[j] * vector[j] for j in range(used))
        weights.append(weight)
        vector = [vector[j] - weight * unit[j] if j < used else vector[j] for j in range(length)]
    square = sum(entry * entry for entry in vector)
    size = jnp.sqrt(square)
    weights.append(size)
    inverse = 1.0 / size
    return weights, [entry * inverse for entry in vector]


def solve_kernel(rows_ref, state_ref, f_ref, v_ref, z_ref, solution_ref, residual_ref):
    state = state_ref[...]
    known = ITERS - 2
    units = [[pick(state, UNIT[k, j]) for j in range(k + 2)] for k in range(known)]
    triangle = {(e, k): pick(state, UPPER[e, k]) for k in range(known) for e in range(k + 1)}
    beta = pick(state, BETA)
    dots = jnp.sum(rows_ref[...], axis=0, keepdims=True)
    gram, products, square = read_dots(dots, state, ITERS)
    heights, _, length = heights_of(gram, products, square, shifts_of(ITERS), ITERS)
    for k in range(known, ITERS):
        if k == ITERS - 1:
            vector = heights + [length]
        else:
            vector = [pick(state, HESS[j, k]) for j in range(k + 2)]
        weights, unit = orthogonalized(vector, units, k + 2)
        units.append(unit)
        triangle.update({(e, k): weights[e] for e in range(k + 1)})
    inverses = [1.0 / triangle[k, k] for k in range(ITERS)]
    answers = [None] * ITERS
    for k in reversed(range(ITERS)):
        running = beta * units[k][0]
        for later in reversed(range(k + 1, ITERS)):
            running = running - triangle[k, later] * answers[later]
        answers[k] = running * inverses[k]
    result = answers[0] * v_ref[0]
    rest = f_ref[...] - answers[0] * z_ref[0]
    for k in range(1, ITERS):
        result = result + answers[k] * v_ref[k]
        rest = rest - answers[k] * z_ref[k]
    solution_ref[...] = result
    residual_ref[...] = rest


def on_device(
    forcing,
    stiffness,
    positions,
    far_weights,
    far_profile,
    near_blocks,
    near_dest,
    near_cilia,
    near_count,
):
    rows = lax.axis_size("row")
    cols = lax.axis_size("col")
    comps, cil, points = forcing.shape
    slots = near_blocks.shape[0]
    width = comps * points
    flat = comps * cil
    total = cil * rows * cols
    struct = lambda *shape, dtype=F32: jax.ShapeDtypeStruct(shape, dtype)
    vmem, smem, hbm = (pl.BlockSpec(memory_space=m) for m in (pltpu.VMEM, pltpu.SMEM, pltpu.HBM))
    slim = pltpu.CompilerParams(vmem_limit_bytes=4 << 20)
    roomy = pltpu.CompilerParams(vmem_limit_bytes=8 << 20)
    f = forcing.reshape(flat, points)
    stiff = stiffness.reshape(1, cil)
    weights = far_weights.reshape(1, points)
    profile = far_profile.reshape(1, points)
    in_hbm = lambda array: pltpu.with_memory_space_constraint(array, pltpu.HBM)
    blocks = in_hbm(near_blocks)
    cilia = in_hbm(near_cilia.T)
    dest = in_hbm(near_dest.reshape(slots))


    def exchange(send, x, kept, first):
        arrived = lax.all_to_all(send, "row", split_axis=0, concat_axis=0, tiled=True)
        outs, specs = [struct(cols, TILE, LANES, dtype=BF16)], [vmem]
        if first:
            table, extra = dest, ()
            outs += [pltpu.VMEM((KEPT, width, width), BF16), struct(slots, dtype=jnp.int32)]
            specs += [vmem, smem]
        else:
            table, extra = in_hbm(kept[1]), kept[:1]
        near, *fetched = pl.pallas_call(
            functools.partial(near_kernel, comps, cil, first),
            out_shape=outs,
            in_specs=[hbm, hbm, smem, vmem, hbm] + [vmem] * len(extra),
            out_specs=specs,
            scratch_shapes=[
                pltpu.VMEM((cil, TILE, width), BF16),
                pltpu.VMEM((cols * TILE, points), F32),
                pltpu.SMEM((cols,), jnp.int32),
                pltpu.VMEM((slots - KEPT, width, width), BF16),
                pltpu.SMEM(cilia.shape, jnp.int32),
                pltpu.SMEM(dest.shape, jnp.int32),
                pltpu.SemaphoreType.DMA((2 * len(CHUNKS),)),
                pltpu.SemaphoreType.DMA((2,)),
            ],
            compiler_params=pltpu.CompilerParams(vmem_limit_bytes=16 << 20),
            name="near",
        )(cilia, table, near_count, x, blocks, *extra)
        out = pl.pallas_call(
            functools.partial(join_kernel, comps, first),
            out_shape=struct(cols, PITCH[first], LANES, dtype=BF16),
            compiler_params=slim,
            name="join",
        )(arrived, near)
        recv = lax.all_to_all(out, "col", split_axis=0, concat_axis=0, tiled=True)
        return recv.reshape(cols * PITCH[first], LANES), fetched if first else kept

    send, x = pl.pallas_call(
        functools.partial(first_kernel, comps, cil),
        out_shape=[struct(rows, TILE, LANES), struct(flat, points)],
        in_specs=[hbm, hbm, hbm],
        out_specs=[vmem, vmem],
        scratch_shapes=[
            pltpu.VMEM((comps, cil), F32),
            pltpu.VMEM((1, points), F32),
            pltpu.SemaphoreType.DMA((comps,)),
        ],
        compiler_params=slim,
        name="first",
    )(in_hbm(f), in_hbm(positions), in_hbm(weights))
    recv, kept = exchange(send, x, None, True)
    sorted_rows = flat + comps * cols + TILE
    for step in range(1, ITERS + 1):
        first, last = step == 1, step == ITERS
        ins = [recv, x, stiff, profile]
        if not last:
            ins.append(weights)
        ins += [positions] if first else [sort, pairs, state, vs, zs]
        outs = []
        if first:
            outs += [
                struct(sorted_rows, cols * PITCH[False], dtype=BF16),
                struct(1 + comps, cols, cil, LANES),
            ]
        outs += [
            struct(rows * cols, LANES) if last else struct(rows, comps + 1, LANES),
            struct(flat, points),
            struct(step, flat, points),
            struct(step, flat, points),
            struct(1, LANES),
        ]
        results = pl.pallas_call(
            functools.partial(krylov_kernel, comps, cil, cols, total, step),
            out_shape=outs,
            scratch_shapes=[pltpu.VMEM((sorted_rows + comps * cols * first, LANES), F32)],
            compiler_params=roomy,
            name="krylov",
        )(*ins)
        if first:
            sort, pairs = results[:2]
            results = results[2:]
        send, x, vs, zs, state = results
        if not last:
            recv, _ = exchange(send, x, kept, False)
    everyone = lax.all_to_all(send, ("row", "col"), split_axis=0, concat_axis=0, tiled=True)
    out, rest = pl.pallas_call(
        solve_kernel, out_shape=[struct(flat, points)] * 2, compiler_params=slim, name="solve"
    )(everyone, state, f, vs, zs)
    return out.reshape(forcing.shape), rest.reshape(forcing.shape)


def solution(mesh):
    in_specs = (
        P(None, ("row", "col"), None),
        P(("row", "col")),
        P(None, ("row", "col")),
        P(),
        P(),
        P(("row", "col"), None, None),
        P(("row", "col"), None),
        P(("row", "col"), None),
        P(("row", "col")),
    )
    out_specs = (P(None, ("row", "col"), None), P(None, ("row", "col"), None))
    return jax.shard_map(
        on_device, mesh=mesh, in_specs=in_specs, out_specs=out_specs, check_vma=False
    )
```

```python
import functools
import jax
import jax.numpy as jnp
from jax import lax
from jax.experimental import pallas as pl
from jax.experimental.pallas import tpu as pltpu
from jax.sharding import PartitionSpec as P

CAPD = 2
ITERS = 4
EPSILON = 1e-06
F32 = jnp.float32
BF16 = jnp.bfloat16
HIGHEST = lax.Precision.HIGHEST
LANES = 128
GRAM = {(j, l): l * (l + 1) // 2 + j for l in range(ITERS) for j in range(l + 1)}
HESS = {(j, k): 16 + 8 * k + j for k in range(ITERS) for j in range(k + 2)}
BETA = 63
UPPER = {(e, k): 64 + 4 * k + e for k in range(ITERS) for e in range(k + 1)}
UNIT = {(k, j): 80 + 8 * k + j for k in range(ITERS) for j in range(k + 2)}
SHIFT = 2.0


def lane_iota(shape):
    return lax.broadcasted_iota(jnp.int32, shape, len(shape) - 1)


def column(row, size):
    eye = lax.broadcasted_iota(jnp.int32, (size, size), 0) == lane_iota((size, size))
    return jnp.sum(jnp.where(eye, row, 0.0), axis=1, keepdims=True)


def tall(col, comps):
    return jnp.concatenate([col] * comps, axis=0)


def bend(x, stiff):
    points = x.shape[1]
    lane = lane_iota(x.shape)

    def shifted(by):
        moved = pltpu.roll(x, by % points, 1)
        keep = lane >= by if by > 0 else lane < points + by
        return jnp.where(keep, moved, 0.0)

    fourth = shifted(2) - 4.0 * shifted(1) + 6.0 * x - 4.0 * shifted(-1) + shifted(-2)
    return x + stiff * fourth


def placed(x, weights, place, comps, cil):
    sums = jnp.sum(x * weights, axis=1, keepdims=True)
    return [
        jnp.sum(sums[i * cil:(i + 1) * cil] * place, axis=0, keepdims=True) for i in range(comps)
    ]


def place_of(cil):
    shape = (cil, LANES)
    own = lax.axis_index("row") * cil + lax.broadcasted_iota(jnp.int32, shape, 0)
    return jnp.where(lane_iota(shape) == own, 1.0, 0.0)


def to_every(send_ref, parts):
    if len(send_ref.shape) == 2:
        send_ref[...] = jnp.broadcast_to(parts[0], send_ref.shape)
        return
    rows = list(parts)
    rows += [jnp.zeros((1, LANES), F32)] * (send_ref.shape[1] - len(rows))
    tile = jnp.concatenate(rows, axis=0)
    send_ref[...] = jnp.broadcast_to(tile[None], send_ref.shape)


def dot_row(pairs):
    rows = [jnp.sum(a * b, axis=0, keepdims=True) for a, b in pairs]
    while len(rows) % 8:
        rows.append(jnp.zeros_like(rows[0]))
    sums = jnp.sum(jnp.concatenate(rows, axis=0), axis=1, keepdims=True)
    shape = (len(rows), LANES)
    eye = lax.broadcasted_iota(jnp.int32, shape, 0) == lane_iota(shape)
    return jnp.sum(jnp.where(eye, sums, 0.0), axis=0, keepdims=True)


def pick(row, lane):
    return jnp.broadcast_to(row[:, lane:lane + 1], row.shape)


def pack(entries):
    lane = lane_iota((1, LANES))
    row = jnp.zeros((1, LANES), F32)
    for where, value in entries.items():
        row = jnp.where(lane == where, value, row)
    return row


def first_kernel(comps, cil, f_hbm, pos_hbm, w_hbm, send_ref, x_out, pos_ref, w_ref, sems):
    copies = [
        pltpu.make_async_copy(source, target, sems.at[n])
        for n, (source, target) in enumerate(((f_hbm, x_out), (pos_hbm, pos_ref), (w_hbm, w_ref)))
    ]
    for copy in copies:
        copy.start()
    place = place_of(cil)
    for copy in copies:
        copy.wait()
    f = x_out[...]
    parts = placed(f, w_ref[...], place, comps, cil)
    parts.append(dot_row([(f, f)]))
    for i in range(comps):
        col = column(pos_ref[i:i + 1, :], cil)
        parts.append(jnp.sum(col * place, axis=0, keepdims=True))
    to_every(send_ref, parts)


TILE = 8
KEPT = 6
CHUNKS = (8, 12, 12)
META = 6
DOTS = 14
PITCH = {True: 24, False: 16}


def near_kernel(comps, cil, first, cilia_hbm, table_hbm, count_ref, x_ref, b_ref, *refs):
    refs = list(refs)
    if not first:
        kept = refs.pop(0)
    out_ref = refs.pop(0)
    if first:
        kept, place_ref = refs[:2]
        refs = refs[2:]
    lhs, result, used, held, cilia_ref, table_ref, sems, table_sems = refs
    points = x_ref.shape[1]
    slots = b_ref.shape[0]
    bounds = [(sum(CHUNKS[:n]), sum(CHUNKS[:n + 1])) for n in range(len(CHUNKS))]

    def block(slot):
        return kept[slot] if slot < KEPT else held[slot - KEPT]

    def fetches(n):
        start, stop = bounds[n]
        parts = []
        if first and start < KEPT:
            parts.append((start, min(stop, KEPT), kept, 0))
        if stop > KEPT:
            parts.append((max(start, KEPT), stop, held, KEPT))
        return [
            pltpu.make_async_copy(
                b_ref.at[pl.ds(begin, end - begin)],
                target.at[pl.ds(begin - offset, end - begin)],
                sems.at[n + (target is kept) * len(CHUNKS)],
            )
            for begin, end, target, offset in parts
        ]

    tables = [
        pltpu.make_async_copy(source, target, table_sems.at[n])
        for n, (source, target) in enumerate(((cilia_hbm, cilia_ref), (table_hbm, table_ref)))
    ]
    for copy in tables:
        copy.start()
    for n in range(len(CHUNKS)):
        for copy in fetches(n):
            copy.start()
    result[...] = jnp.zeros_like(result)
    x = x_ref[...]
    high = x.astype(BF16).astype(F32)
    low = x - high
    row = lax.broadcasted_iota(jnp.int32, (TILE, points), 0)
    for g in range(cil):
        for i in range(comps):
            at = i * cil + g
            value = jnp.where(row == 0, high[at:at + 1], jnp.where(row == 1, low[at:at + 1], 0.0))
            lhs[g, :, i * points:(i + 1) * points] = value.astype(BF16)
    for copy in tables:
        copy.wait()
    if first:
        lane = lane_iota((1, points))
        for dest in range(used.shape[0]):
            used[dest] = 0
        for slot in range(slots):
            dest = table_ref[slot]
            rank = used[dest]
            used[dest] = rank + 1
            place_ref[slot] = dest * TILE + rank * comps
            at = pl.ds(dest * TILE + META, 1)
            target = cilia_ref[1, slot].astype(F32)
            result[at, :] = jnp.where(lane == rank, target, result[at, :])
    else:
        place_ref = table_ref
    for n, (start, stop) in enumerate(bounds):
        for copy in fetches(n):
            copy.wait()
        speeds = [
            lax.dot_general(
                lhs[cilia_ref[0, slot]], block(slot), (((1,), (1,)), ((), ())),
                preferred_element_type=F32,
            )
            for slot in range(start, stop)
        ]
        for slot, speed in zip(range(start, stop), speeds):
            speed = jnp.where(slot < count_ref[0], speed[0:1] + speed[1:2], 0.0)
            for i in range(comps):
                result[pl.ds(place_ref[slot] + i, 1), :] = speed[:, i * points:(i + 1) * points]
    out_ref[...] = result[...].astype(BF16).reshape(out_ref.shape)


def join_kernel(comps, first, rows_ref, near_ref, send_ref):
    total = jnp.sum(rows_ref[...], axis=0)
    high = total.astype(BF16).astype(F32)
    rest = total - high
    middle = rest.astype(BF16).astype(F32)
    low = rest - middle
    at = comps
    shared = jnp.concatenate(
        [
            high[:at], rest[:at], high[at:at + 1],
            middle[at:at + 1] + pltpu.roll(low[at:at + 1], LANES // 2, 1),
        ],
        axis=0,
    )
    send_ref[:, :TILE, :] = near_ref[...]
    send_ref[:, TILE:2 * TILE, :] = jnp.broadcast_to(
        shared.astype(BF16)[None], (send_ref.shape[0],) + shared.shape
    )
    if first:
        at = comps + 1
        places = jnp.concatenate(
            [high[at:at + comps], rest[at:at + comps], jnp.zeros((TILE - 2 * comps, LANES), F32)], axis=0
        )
        send_ref[:, 2 * TILE:3 * TILE, :] = jnp.broadcast_to(
            places.astype(BF16)[None], (send_ref.shape[0],) + places.shape
        )


def sorting(comps, cil, sources, pitch, targets):
    def parts(rows):
        shape = (rows, sources * pitch)
        row = lax.broadcasted_iota(jnp.int32, shape, 0)
        lane = lane_iota(shape)
        return row, lax.div(lane, pitch), lax.rem(lane, pitch)

    row, _, place = parts(comps * cil)
    comp, cilium = lax.div(row, cil), lax.rem(row, cil).astype(F32)
    found = jnp.zeros(row.shape, jnp.bool_)
    for rank in range(CAPD):
        found |= (place == rank * comps + comp) & (cilium == targets[rank])
    pieces = [found]

    def gathered(start):
        row, source, place = parts(comps * sources)
        comp, wanted = lax.div(row, sources), lax.rem(row, sources)
        here = (place == start + comp) | (place == start + comps + comp)
        return here & (source == wanted)

    pieces.append(gathered(TILE))
    row, _, place = parts(TILE)
    pieces.append((row == 0) & ((place == DOTS) | (place == DOTS + 1)))
    if pitch > 2 * TILE:
        pieces.append(gathered(2 * TILE))
    return jnp.concatenate([jnp.where(p, 1.0, 0.0) for p in pieces], axis=0).astype(BF16)


def applied(x, stiff, rows, pairs, profile, comps, cil, sources):
    flat = comps * cil
    image = bend(x, stiff) + rows[:flat]
    totals = [jnp.zeros((cil, LANES), F32) for _ in range(comps)]
    for s in range(sources):
        strength = [rows[flat + j * sources + s:flat + j * sources + s + 1] for j in range(comps)]
        along = [pairs(1 + j, s) for j in range(comps)]
        projected = sum(along[j] * strength[j] for j in range(comps))
        direct = pairs(0, s)
        for i in range(comps):
            totals[i] = totals[i] + (direct * strength[i] + along[i] * projected)
    far = jnp.concatenate([jnp.sum(t, axis=1, keepdims=True) for t in totals], axis=0)
    dots = rows[flat + comps * sources:flat + comps * sources + 1]
    dots = dots + pltpu.roll(dots, LANES // 2, 1)
    return image + far * profile, dots


def krylov_kernel(comps, cil, sources, total, step, *refs):
    first = step == 1
    last = step == ITERS
    refs = list(refs)
    recv_ref, x_ref, stiff_ref, prof_ref = refs[:4]
    refs = refs[4:]
    if not last:
        w_ref = refs.pop(0)
    if first:
        pos_ref = refs.pop(0)
    else:
        sort_ref, pairs_ref, state_ref, v_ref, z_ref = refs[:5]
        refs = refs[5:]
    if first:
        sort_out, pairs_out = refs[:2]
        refs = refs[2:]
    send_ref, x_out, v_out, z_out, state_out, rows = refs
    x = x_ref[...]
    flat = comps * cil
    stiff = tall(column(stiff_ref[...], cil), comps)

    if first:
        pitch = PITCH[True]
        arrived = recv_ref[...]
        shape = (sources, sources * pitch)
        source, lane = lax.broadcasted_iota(jnp.int32, shape, 0), lane_iota(shape)
        chosen = jnp.where(lane == source * pitch + META, 1.0, 0.0).astype(BF16)
        meta = jnp.dot(chosen, arrived, preferred_element_type=F32)
        eye = lax.broadcasted_iota(jnp.int32, (sources, sources), 0) == lane_iota((sources, sources))
        named = [
            jnp.sum(jnp.where(eye, meta[:, rank:rank + 1], 0.0), axis=0, keepdims=True) for rank in range(CAPD)
        ]
        named = jnp.concatenate(
            [jnp.broadcast_to(n, (TILE, sources)) for n in named], axis=0
        ).astype(BF16)

        def targets_for(pitch):
            shape = (sources, sources * pitch)
            source, lane = lax.broadcasted_iota(jnp.int32, shape, 0), lane_iota(shape)
            spread = jnp.where(lax.div(lane, pitch) == source, 1.0, 0.0).astype(BF16)
            wide = jnp.dot(named, spread, preferred_element_type=F32)
            return [wide[rank * TILE:rank * TILE + 1] for rank in range(CAPD)]

        sort_out[...] = sorting(comps, cil, sources, PITCH[False], targets_for(PITCH[False]))
        sort = sorting(comps, cil, sources, pitch, targets_for(pitch))
        rows[...] = jnp.dot(sort, arrived, preferred_element_type=F32)
        eps_three = 4.0 / total
        eps_two = eps_three ** (2.0 / 3.0)
        here = [
            jnp.broadcast_to(column(pos_ref[i:i + 1, :], cil), (cil, LANES)) for i in range(comps)
        ]
        start = flat + comps * sources + TILE
        for s in range(sources):
            gap = [
                here[i] - rows[start + i * sources + s:start + i * sources + s + 1]
                for i in range(comps)
            ]
            inverse = 1.0 / (gap[0] * gap[0] + gap[1] * gap[1] + gap[2] * gap[2] + eps_two)
            amplitude = eps_three * inverse * jnp.sqrt(inverse)
            slope = jnp.sqrt(amplitude * inverse)
            pairs_out[0, s] = amplitude
            for i in range(comps):
                pairs_out[1 + i, s] = slope * gap[i]
        pairs = lambda at, s: pairs_out[at, s]
    else:
        rows[...] = jnp.dot(sort_ref[...], recv_ref[...], preferred_element_type=F32)
        pairs = lambda at, s: pairs_ref[at, s]

    image, dots = applied(x, stiff, rows, pairs, prof_ref[...], comps, cil, sources)
    entries = {}
    if first:
        beta = jnp.sqrt(pick(dots, 0) + EPSILON)
        entries[BETA] = beta
        scale = 1.0 / beta
        basis = [x * scale]
        images = [image * scale]
    else:
        state = state_ref[...]
        count = step - 1
        gram, products, square = read_dots(dots, state, count)
        basis = [v_ref[j] for j in range(count)]
        images = [z_ref[j] for j in range(count)]
        heights, taken, length = heights_of(gram, products, square, shifts_of(count), count)
        scale = 1.0 / length
        vector, product = x, image
        for j in range(count):
            vector = vector - taken[j] * basis[j]
            product = product - taken[j] * images[j]
        basis.append(vector * scale)
        images.append(product * scale)
        for j in range(count):
            entries[GRAM[j, count - 1]] = gram[j, count - 1]
            entries[HESS[j, count - 1]] = heights[j]
        entries[HESS[count, count - 1]] = length
        if last:
            units = []
            for k in range(count - 1):
                vector = [pick(state, HESS[j, k]) for j in range(k + 2)]
                weights, unit = orthogonalized(vector, units, k + 2)
                units.append(unit)
                entries.update({UPPER[e, k]: weights[e] for e in range(k + 1)})
                entries.update({UNIT[k, j]: unit[j] for j in range(k + 2)})
    row = pack(entries)
    state_out[...] = row if first else row + state
    for j in range(step):
        v_out[j] = basis[j]
        z_out[j] = images[j]
    outgoing = images[-1]
    for j, shift in enumerate(shifts_of(step)):
        if shift:
            outgoing = outgoing - shift * basis[j]
    pairs_of_dots = [(basis[j], basis[-1]) for j in range(step)]
    pairs_of_dots += [(basis[j], outgoing) for j in range(step)]
    pairs_of_dots.append((outgoing, outgoing))
    local = dot_row(pairs_of_dots)
    if last:
        to_every(send_ref, [local])
    else:
        to_every(send_ref, placed(outgoing, w_ref[...], place_of(cil), comps, cil) + [local])
    x_out[...] = outgoing


def shifts_of(count):
    if count == ITERS:
        return [0.0] * count
    return [0.0] * (count - 1) + [SHIFT]


def read_dots(dots, state, count):
    gram = {}
    for l in range(count):
        for j in range(l + 1):
            gram[j, l] = pick(dots, j) if l == count - 1 else pick(state, GRAM[j, l])
            gram[l, j] = gram[j, l]
    return gram, [pick(dots, count + j) for j in range(count)], pick(dots, 2 * count)


def heights_of(gram, products, square, shifts, count):
    heights, taken = [], []
    for j in range(count):
        extra = sum((shifts[l] * gram[j, l] for l in range(count) if shifts[l]), 0.0)
        heights.append(products[j] + extra)
        taken.append(heights[j] - shifts[j])
    norm = square
    for j in range(count):
        inner = -2.0 * products[j]
        for l in range(count):
            inner = inner + taken[l] * gram[j, l]
        norm = norm + taken[j] * inner
    return heights, taken, jnp.sqrt(jnp.maximum(norm, 0.0) + EPSILON)


def orthogonalized(vector, units, length):
    weights = []
    for e, unit in enumerate(units):
        used = min(e + 2, length)
        weight = sum(unit[j] * vector[j] for j in range(used))
        weights.append(weight)
        vector = [vector[j] - weight * unit[j] if j < used else vector[j] for j in range(length)]
    square = sum(entry * entry for entry in vector)
    size = jnp.sqrt(square)
    weights.append(size)
    inverse = 1.0 / size
    return weights, [entry * inverse for entry in vector]


def solve_kernel(rows_ref, state_ref, f_ref, v_ref, z_ref, solution_ref, residual_ref):
    state = state_ref[...]
    known = ITERS - 2
    units = [[pick(state, UNIT[k, j]) for j in range(k + 2)] for k in range(known)]
    triangle = {(e, k): pick(state, UPPER[e, k]) for k in range(known) for e in range(k + 1)}
    beta = pick(state, BETA)
    dots = jnp.sum(rows_ref[...], axis=0, keepdims=True)
    gram, products, square = read_dots(dots, state, ITERS)
    heights, _, length = heights_of(gram, products, square, shifts_of(ITERS), ITERS)
    for k in range(known, ITERS):
        if k == ITERS - 1:
            vector = heights + [length]
        else:
            vector = [pick(state, HESS[j, k]) for j in range(k + 2)]
        weights, unit = orthogonalized(vector, units, k + 2)
        units.append(unit)
        triangle.update({(e, k): weights[e] for e in range(k + 1)})
    inverses = [1.0 / triangle[k, k] for k in range(ITERS)]
    answers = [None] * ITERS
    for k in reversed(range(ITERS)):
        running = beta * units[k][0]
        for later in reversed(range(k + 1, ITERS)):
            running = running - triangle[k, later] * answers[later]
        answers[k] = running * inverses[k]
    result = answers[0] * v_ref[0]
    rest = f_ref[...] - answers[0] * z_ref[0]
    for k in range(1, ITERS):
        result = result + answers[k] * v_ref[k]
        rest = rest - answers[k] * z_ref[k]
    solution_ref[...] = result
    residual_ref[...] = rest


def on_device(
    forcing,
    stiffness,
    positions,
    far_weights,
    far_profile,
    near_blocks,
    near_dest,
    near_cilia,
    near_count,
):
    rows = lax.axis_size("row")
    cols = lax.axis_size("col")
    comps, cil, points = forcing.shape
    slots = near_blocks.shape[0]
    width = comps * points
    flat = comps * cil
    total = cil * rows * cols
    struct = lambda *shape, dtype=F32: jax.ShapeDtypeStruct(shape, dtype)
    vmem, smem, hbm = (pl.BlockSpec(memory_space=m) for m in (pltpu.VMEM, pltpu.SMEM, pltpu.HBM))
    slim = pltpu.CompilerParams(vmem_limit_bytes=4 << 20)
    roomy = pltpu.CompilerParams(vmem_limit_bytes=8 << 20)
    f = forcing.reshape(flat, points)
    stiff = stiffness.reshape(1, cil)
    weights = far_weights.reshape(1, points)
    profile = far_profile.reshape(1, points)
    in_hbm = lambda array: pltpu.with_memory_space_constraint(array, pltpu.HBM)
    blocks = in_hbm(near_blocks)
    cilia = in_hbm(near_cilia.T)
    dest = in_hbm(near_dest.reshape(slots))


    def exchange(send, x, kept, first):
        arrived = lax.all_to_all(send, "row", split_axis=0, concat_axis=0, tiled=True)
        outs, specs = [struct(cols, TILE, LANES, dtype=BF16)], [vmem]
        if first:
            table, extra = dest, ()
            outs += [pltpu.VMEM((KEPT, width, width), BF16), struct(slots, dtype=jnp.int32)]
            specs += [vmem, smem]
        else:
            table, extra = in_hbm(kept[1]), kept[:1]
        near, *fetched = pl.pallas_call(
            functools.partial(near_kernel, comps, cil, first),
            out_shape=outs,
            in_specs=[hbm, hbm, smem, vmem, hbm] + [vmem] * len(extra),
            out_specs=specs,
            scratch_shapes=[
                pltpu.VMEM((cil, TILE, width), BF16),
                pltpu.VMEM((cols * TILE, points), F32),
                pltpu.SMEM((cols,), jnp.int32),
                pltpu.VMEM((slots - KEPT, width, width), BF16),
                pltpu.SMEM(cilia.shape, jnp.int32),
                pltpu.SMEM(dest.shape, jnp.int32),
                pltpu.SemaphoreType.DMA((2 * len(CHUNKS),)),
                pltpu.SemaphoreType.DMA((2,)),
            ],
            compiler_params=pltpu.CompilerParams(vmem_limit_bytes=16 << 20),
            name="near",
        )(cilia, table, near_count, x, blocks, *extra)
        out = pl.pallas_call(
            functools.partial(join_kernel, comps, first),
            out_shape=struct(cols, PITCH[first], LANES, dtype=BF16),
            compiler_params=slim,
            name="join",
        )(arrived, near)
        recv = lax.all_to_all(out, "col", split_axis=0, concat_axis=0, tiled=True)
        return recv.reshape(cols * PITCH[first], LANES), fetched if first else kept

    send, x = pl.pallas_call(
        functools.partial(first_kernel, comps, cil),
        out_shape=[struct(rows, TILE, LANES), struct(flat, points)],
        in_specs=[hbm, hbm, hbm],
        out_specs=[vmem, vmem],
        scratch_shapes=[
            pltpu.VMEM((comps, cil), F32),
            pltpu.VMEM((1, points), F32),
            pltpu.SemaphoreType.DMA((comps,)),
        ],
        compiler_params=slim,
        name="first",
    )(in_hbm(f), in_hbm(positions), in_hbm(weights))
    recv, kept = exchange(send, x, None, True)
    sorted_rows = flat + comps * cols + TILE
    for step in range(1, ITERS + 1):
        first, last = step == 1, step == ITERS
        ins = [recv, x, stiff, profile]
        if not last:
            ins.append(weights)
        ins += [positions] if first else [sort, pairs, state, vs, zs]
        outs = []
        if first:
            outs += [
                struct(sorted_rows, cols * PITCH[False], dtype=BF16),
                struct(1 + comps, cols, cil, LANES),
            ]
        outs += [
            struct(rows * cols, LANES) if last else struct(rows, TILE, LANES),
            struct(flat, points),
            struct(step, flat, points),
            struct(step, flat, points),
            struct(1, LANES),
        ]
        results = pl.pallas_call(
            functools.partial(krylov_kernel, comps, cil, cols, total, step),
            out_shape=outs,
            scratch_shapes=[pltpu.VMEM((sorted_rows + comps * cols * first, LANES), F32)],
            compiler_params=roomy,
            name="krylov",
        )(*ins)
        if first:
            sort, pairs = results[:2]
            results = results[2:]
        send, x, vs, zs, state = results
        if not last:
            recv, _ = exchange(send, x, kept, False)
    everyone = lax.all_to_all(send, ("row", "col"), split_axis=0, concat_axis=0, tiled=True)
    out, rest = pl.pallas_call(
        solve_kernel, out_shape=[struct(flat, points)] * 2, compiler_params=slim, name="solve"
    )(everyone, state, f, vs, zs)
    return out.reshape(forcing.shape), rest.reshape(forcing.shape)


def solution(mesh):
    in_specs = (
        P(None, ("row", "col"), None),
        P(("row", "col")),
        P(None, ("row", "col")),
        P(),
        P(),
        P(("row", "col"), None, None),
        P(("row", "col"), None),
        P(("row", "col"), None),
        P(("row", "col")),
    )
    out_specs = (P(None, ("row", "col"), None), P(None, ("row", "col"), None))
    return jax.shard_map(
        on_device, mesh=mesh, in_specs=in_specs, out_specs=out_specs, check_vma=False
    )
```
